32 devices in a mesh: ctx: 4 (over y, x), fsdp: 8 (over z, core).
Axes of the slice: x: 2, y: 2, z: 4, core: 2. Of those that a mesh axis runs over, the one named last changes fastest.
Arguments:
- tokens: bfloat16 [2, 8, 1024, 1024], P(None, 'fsdp', 'ctx'), may hold values from -6 to 6
- doc_lengths: int32 [2, 8, 4], P(None, 'fsdp'), may hold values from 1 to 512, 1024 in all within a row
- w_query: bfloat16 [1024, 1024], P(('ctx', 'fsdp')), may hold values from -0.1875 to 0.1875
- b_query: bfloat16 [1024], P(('ctx', 'fsdp')), may hold values from -1.75 to 1.75
- w_key: bfloat16 [1024, 1024], P(('ctx', 'fsdp')), may hold values from -0.1875 to 0.1875
- w_value: bfloat16 [1024, 1024], P(('ctx', 'fsdp')), may hold values from -0.1875 to 0.1875
- b_value: bfloat16 [1024], P(('ctx', 'fsdp')), may hold values from -0.3125 to 0.3125
- w_out: bfloat16 [1024, 1024], P(('ctx', 'fsdp')), may hold values from -1.5 to 1.5
- b_out: bfloat16 [1024], P(('ctx', 'fsdp')), may hold values from -1.75 to 1.75
- ln1_gain: bfloat16 [1024], P(('ctx', 'fsdp')), may hold values from 0.5 to 1.5
- ln1_bias: bfloat16 [1024], P(('ctx', 'fsdp')), may hold values from -1.75 to 1.75
- w_up: bfloat16 [1024, 4096], P(('ctx', 'fsdp')), may hold values from -0.1875 to 0.1875
- b_up: bfloat16 [4096], P(('ctx', 'fsdp')), may hold values from -1.75 to 1.75
- w_down: bfloat16 [4096, 1024], P(('ctx', 'fsdp')), may hold values from -0.09375 to 0.09375
- b_down: bfloat16 [1024], P(('ctx', 'fsdp')), may hold values from -1.75 to 1.75
- ln2_gain: bfloat16 [1024], P(('ctx', 'fsdp')), may hold values from 0.5 to 1.5
- ln2_bias: bfloat16 [1024], P(('ctx', 'fsdp')), may hold values from -1.75 to 1.75
- cotangent: bfloat16 [2, 8, 1024, 1024], P(None, 'fsdp', 'ctx'), may hold values from -6 to 6
Outputs:
- output: bfloat16 [2, 8, 1024, 1024], P(None, 'fsdp', 'ctx')
- grad_tokens: float32 [2, 8, 1024, 1024], P(None, 'fsdp', 'ctx')
- grad_w_query: float32 [1024, 1024], P(('ctx', 'fsdp'))
- grad_b_query: float32 [1024], P(('ctx', 'fsdp'))
- grad_w_key: float32 [1024, 1024], P(('ctx', 'fsdp'))
- grad_w_value: float32 [1024, 1024], P(('ctx', 'fsdp'))
- grad_b_value: float32 [1024], P(('ctx', 'fsdp'))
- grad_w_out: float32 [1024, 1024], P(('ctx', 'fsdp'))
- grad_b_out: float32 [1024], P(('ctx', 'fsdp'))
- grad_ln1_gain: float32 [1024], P(('ctx', 'fsdp'))
- grad_ln1_bias: float32 [1024], P(('ctx', 'fsdp'))
- grad_w_up: float32 [1024, 4096], P(('ctx', 'fsdp'))
- grad_b_up: float32 [4096], P(('ctx', 'fsdp'))
- grad_w_down: float32 [4096, 1024], P(('ctx', 'fsdp'))
- grad_b_down: float32 [1024], P(('ctx', 'fsdp'))
- grad_ln2_gain: float32 [1024], P(('ctx', 'fsdp'))
- grad_ln2_bias: float32 [1024], P(('ctx', 'fsdp'))
The draws below stay inside these ranges and needn't reach their ends.
Inputs may be any that keep to these rules, and one draw needn't show every extreme that they name: `doc_lengths`: in each stream the 4 documents fill the 1024 positions in order, and the longest is exactly 512.
All inputs are finite; a program needn't handle non-finite values.
Results may differ from the reference program's by a relative error of at most 0.014.
Values may be sent and summed in bfloat16 or wider, within the bound.
No kernel may reach another device: no remote copies, remote signals or barrier semaphores. Data moves between devices by JAX's collectives and lax.ppermute only.
A program may use at most 256 MiB of HBM per device.

```python
import math
import jax
import jax.numpy as jnp
import numpy as np
from jax import lax

D = 1024
H = 16
HD = 64
FF = 4096
MB = 2
STREAMS = 8
LEN = 1024
DOC_MAX = 512
NDOC = 4


def levels(stream_key, shape, split, low, high):
    level, own = 1.0, jax.random.fold_in(stream_key, 6)
    for dim, blocks in split:
        heights = jnp.exp(jax.random.uniform(jax.random.fold_in(own, dim), (blocks,), jnp.float32, low / len(split), high / len(split)))
        level = level * jnp.repeat(heights, shape[dim] // blocks).reshape([-1 if axis == dim else 1 for axis in range(len(shape))])
    return level


def split_up(count, total, limit, lean):
    weights = [(1 << 20) // math.isqrt(standing ** lean) + 1 for standing in range(2, count + 1)]
    rest, counts = total - limit - (count - 1), [1] * (count - 1)
    while rest > 0:
        candidates = [i for i in range(count - 1) if counts[i] < limit]
        mass, remaining = sum([weights[i] for i in candidates]), rest
        for i in candidates:
            more = min(limit - counts[i], max(1, remaining * weights[i] // mass), rest)
            counts[i] = counts[i] + more
            rest = rest - more
    return np.array([limit] + counts)


def ragged(rng, amount, total, reach, lean):
    if amount == 2:
        one = jax.random.randint(rng, (), max(1, total - reach), min(reach, total - 1) + 1)
        return jnp.stack([one, total - one])
    sizes = jnp.asarray(split_up(amount, total, reach, lean), jnp.int32)
    couples = (amount - 1) // 2
    source_of, taker = sizes[1:1 + 2 * couples:2], sizes[2:2 + 2 * couples:2]
    room = jnp.minimum(source_of - 1, reach - taker)
    moved = jax.random.randint(jax.random.fold_in(rng, 1), (couples,), 0, 1 << 20) % (room + 1)
    sizes = sizes.at[1:1 + 2 * couples:2].set(source_of - moved).at[2:2 + 2 * couples:2].set(taker + moved)
    return sizes[jax.random.permutation(jax.random.fold_in(rng, 2), amount)]


def scatter_about(own_key, extent, scale, most, cuts=(), held_as=jnp.bfloat16):
    level = levels(own_key, extent, cuts, -0.22, 0.18) if cuts else 1.0
    values = jax.random.normal(own_key, extent, jnp.float32) * scale * level
    return jnp.minimum(jnp.maximum(values, -most), most).astype(held_as)


def setup_inputs(seed: int = 0) -> dict:
    key_list = jax.random.split(jax.random.key(seed), 19)
    return {
        "tokens": scatter_about(key_list[0], (MB, STREAMS, LEN, D), 1.0, 6.0, ((1, 8), (2, 4))),
        "doc_lengths": jax.vmap(lambda own: ragged(own, NDOC, LEN, DOC_MAX, 2))(jax.random.split(key_list[1], MB * STREAMS)).reshape((MB, STREAMS, NDOC)).astype(jnp.int32),
        "w_query": scatter_about(key_list[2], (D, D), D ** -0.5, 0.1875, ((0, 32),)),
        "b_query": scatter_about(key_list[3], (D,), 0.3, 1.75, ((0, 32),)),
        "w_key": scatter_about(key_list[4], (D, D), D ** -0.5, 0.1875, ((0, 32),)),
        "w_value": scatter_about(key_list[5], (D, D), D ** -0.5, 0.1875, ((0, 32),)),
        "b_value": scatter_about(key_list[6], (D,), 0.05, 0.3125, ((0, 32),)),
        "w_out": scatter_about(key_list[7], (D, D), (D // 64) ** -0.5, 1.5, ((0, 32),)),
        "b_out": scatter_about(key_list[8], (D,), 0.3, 1.75, ((0, 32),)),
        "ln1_gain": jnp.clip(1.0 + 0.1 * jax.random.normal(key_list[9], (D,), jnp.float32), 0.5, 1.5).astype(jnp.bfloat16),
        "ln1_bias": scatter_about(key_list[10], (D,), 0.3, 1.75, ((0, 32),)),
        "w_up": scatter_about(key_list[11], (D, FF), D ** -0.5, 0.1875, ((0, 32),)),
        "b_up": scatter_about(key_list[12], (FF,), 0.3, 1.75, ((0, 32),)),
        "w_down": scatter_about(key_list[13], (FF, D), FF ** -0.5, 0.09375, ((0, 32),)),
        "b_down": scatter_about(key_list[14], (D,), 0.3, 1.75, ((0, 32),)),
        "ln2_gain": jnp.clip(1.0 + 0.1 * jax.random.normal(key_list[15], (D,), jnp.float32), 0.5, 1.5).astype(jnp.bfloat16),
        "ln2_bias": scatter_about(key_list[16], (D,), 0.3, 1.75, ((0, 32),)),
        "cotangent": scatter_about(key_list[17], (MB, STREAMS, LEN, D), 1.0, 6.0, ((1, 8), (2, 4))),
    }


EPSILON = 1e-12
SCORE_SCALE = 0.125
MASKED_SCORE = -1e+30

@jax.custom_vjp
def low(v):
    return lax.optimization_barrier(v.astype(jnp.bfloat16)).astype(jnp.float32)

@jax.custom_vjp
def low_back(v):
    return v

def low_keep(v):
    return (low(v), None)

def low_pass(kept, grad):
    return (grad,)

def back_keep(v):
    return (v, None)

def back_low(kept, grad):
    return (low(grad),)
low.defvjp(low_keep, low_pass)
low_back.defvjp(back_keep, back_low)

def matmul(left, right):
    return jnp.dot(left, right, precision=lax.Precision.HIGHEST)

def layer_norm(values_in, gain_vec, bias_vec):
    center = values_in - lax.optimization_barrier(jnp.mean(values_in, axis=-1, keepdims=True))
    inverse = lax.rsqrt(lax.optimization_barrier(jnp.mean(center * center, axis=-1, keepdims=True)) + EPSILON)
    return center * inverse * gain_vec + bias_vec

def segment_ids(lengths, positions):
    starts = jnp.cumsum(lengths) - lengths
    return lax.optimization_barrier(jnp.sum((positions[:, None] >= starts[None, :]).astype(jnp.int32), axis=1)) - 1

def layer(inputs, weights, segs):
    query_mat, query_bias, key_mat, value_mat, value_bias, out_mat, out_bias, gain_one, bias_one, up_mat, up_bias, down_mat, down_bias, gain_two, bias_two = weights
    queries = low(low_back(matmul(inputs, query_mat) + query_bias))
    keys_all = low(low_back(matmul(inputs, key_mat)))
    values_all = low(low_back(matmul(inputs, value_mat) + value_bias))
    heads_query = queries.reshape(LEN, H, HD)
    heads_key = keys_all.reshape(LEN, H, HD)
    heads_value = values_all.reshape(LEN, H, HD)
    scores = jnp.einsum('qhd,khd->hqk', heads_query, heads_key, precision=lax.Precision.HIGHEST) * SCORE_SCALE
    scores = low_back(jnp.where((segs[:, None] == segs[None, :])[None], scores, MASKED_SCORE))
    probs = low(jax.nn.softmax(scores, axis=-1))
    mixed = jnp.einsum('hqk,khd->qhd', probs, heads_value, precision=lax.Precision.HIGHEST).reshape(LEN, D)
    mixed = low(low_back(mixed))
    attended = low_back(matmul(mixed, out_mat) + out_bias)
    first = layer_norm(inputs + attended, gain_one, bias_one)
    hidden = low_back(matmul(low(first), up_mat) + up_bias)
    activated = low(jax.nn.gelu(hidden, approximate=False))
    branch = low_back(matmul(activated, down_mat) + down_bias)
    return layer_norm(first + branch, gain_two, bias_two)

def reference(tokens, doc_lengths, w_query, b_query, w_key, w_value, b_value, w_out, b_out, ln1_gain, ln1_bias, w_up, b_up, w_down, b_down, ln2_gain, ln2_bias, cotangent):
    params = tuple((item.astype(jnp.float32) for item in (w_query, b_query, w_key, w_value, b_value, w_out, b_out, ln1_gain, ln1_bias, w_up, b_up, w_down, b_down, ln2_gain, ln2_bias)))
    streams_all = MB * STREAMS
    inputs = tokens.astype(jnp.float32).reshape(streams_all, LEN, D)
    grads_in = cotangent.astype(jnp.float32).reshape(streams_all, LEN, D)
    lengths = doc_lengths.reshape(streams_all, NDOC).astype(jnp.int32)

    def one_stream(carry, operands):
        inputs_one, grad_one, lengths_one = operands
        segs = segment_ids(lengths_one, jnp.arange(LEN, dtype=jnp.int32))

        def apply_layer(values_in, weights_in):
            return layer(values_in, weights_in, segs)
        result, pull = jax.vjp(apply_layer, inputs_one, params)
        grad_inputs, grad_weights = pull(grad_one)
        return (jax.tree.map(jnp.add, carry, grad_weights), (result.astype(jnp.bfloat16), grad_inputs))
    initial = tuple((jnp.zeros_like(item) for item in params))
    totals, (results, grad_inputs) = lax.scan(one_stream, initial, (inputs, grads_in, lengths))
    return (results.reshape(MB, STREAMS, LEN, D), grad_inputs.reshape(MB, STREAMS, LEN, D), totals[0], totals[1], totals[2], totals[3], totals[4], totals[5], totals[6], totals[7], totals[8], totals[9], totals[10], totals[11], totals[12], totals[13], totals[14])
```

```python
import functools

import jax
import jax.numpy as jnp
from jax import lax
from jax.experimental import pallas as pl
from jax.experimental.pallas import tpu as pltpu
from jax.sharding import PartitionSpec as P

H = 16
HD = 64
EPSILON = 1e-12
SCORE_SCALE = 0.125
MASKED = -1e30
BF = jnp.bfloat16
F32 = jnp.float32
BOTH = ("ctx", "fsdp")
VMEM_LIMIT = 48 << 20


def dot(a, b, ca, cb):
    return lax.dot_general(a, b, (((ca,), (cb,)), ((), ())), preferred_element_type=F32)


def swap(x, axis, r):
    n = lax.axis_size(axis)
    return lax.ppermute(x, axis, [(i, i ^ r) for i in range(n)])


def bits_of(n):
    return [1 << b for b in range(n.bit_length() - 1)]


def place(pieces, me):
    n = len(pieces)
    out = jnp.zeros((n,) + pieces[0].shape, pieces[0].dtype)
    for r in range(n):
        out = lax.dynamic_update_index_in_dim(out, pieces[r], me ^ r, 0)
    return out


def gather_z(x):
    n = lax.axis_size("fsdp") // 2
    z = lax.axis_index("fsdp") // 2
    pieces = [x] + [swap(x, "fsdp", 2 * r) for r in range(1, n)]
    return place(pieces, z)


def gather_ctx(x, order):
    n = lax.axis_size("ctx")
    pieces = {0: x}
    for b in order:
        for r in list(pieces):
            pieces[r ^ b] = swap(pieces[r], "ctx", b)
    return place([pieces[r] for r in range(n)], lax.axis_index("ctx"))


def scatter_ctx(x, order):
    n = lax.axis_size("ctx")
    me = lax.axis_index("ctx")
    pieces = {r: lax.dynamic_index_in_dim(x, me ^ r, 0, False) for r in range(n)}
    for b in order:
        for r in [r for r in pieces if r & b]:
            got = swap(pieces.pop(r).astype(BF), "ctx", b)
            pieces[r ^ b] = pieces[r ^ b].astype(F32) + got.astype(F32)
    return pieces[0]


def scatter_z(x):
    n = lax.axis_size("fsdp") // 2
    z = lax.axis_index("fsdp") // 2
    x = x.astype(BF)
    total = lax.dynamic_index_in_dim(x, z, 0, False).astype(F32)
    for r in range(1, n):
        got = swap(lax.dynamic_index_in_dim(x, z ^ r, 0, False), "fsdp", 2 * r)
        total = total + got.astype(F32)
    return total


def exchange_ctx(x):
    n = lax.axis_size("ctx")
    me = lax.axis_index("ctx")
    pieces = [lax.dynamic_index_in_dim(x, me, 0, False)]
    for r in range(1, n):
        pieces.append(swap(lax.dynamic_index_in_dim(x, me ^ r, 0, False), "ctx", r))
    return place(pieces, me)


def core_swap(x):
    return swap(x, "fsdp", 1)


def attend_kernel(q_ref, k_ref, v_ref, srow_ref, scol_ref, o_ref, lse_ref):
    q = q_ref[...] * jnp.asarray(SCORE_SCALE, BF)
    s = dot(k_ref[...], q, 0, 0)
    s = jnp.where(scol_ref[...] == srow_ref[...], s, MASKED)
    top = jnp.max(s, axis=0, keepdims=True)
    p = jnp.exp(s - top)
    total = jnp.sum(p, axis=0, keepdims=True)
    o = dot(v_ref[...], p.astype(BF), 1, 0)
    o_ref[...] = (o / total).astype(BF)[None]
    lse_ref[...] = (top + jnp.log(total))[None]


def attend(qkv, seg, block):
    rows, length = qkv.shape
    heads = rows // (3 * HD)
    nq = length // block
    whole = lambda part: pl.BlockSpec((HD, length), lambda h, i: (part * heads + h, 0))
    return pl.pallas_call(
        attend_kernel,
        grid=(heads, nq),
        in_specs=[
            pl.BlockSpec((HD, block), lambda h, i: (h, i)),
            whole(1),
            whole(2),
            pl.BlockSpec((1, block), lambda h, i: (0, i)),
            pl.BlockSpec((length, 1), lambda h, i: (0, 0)),
        ],
        out_specs=[
            pl.BlockSpec((1, HD, block), lambda h, i: (i, h, 0)),
            pl.BlockSpec((1, 1, block), lambda h, i: (h, 0, i)),
        ],
        out_shape=[
            jax.ShapeDtypeStruct((nq, heads * HD, block), BF),
            jax.ShapeDtypeStruct((heads, 1, length), F32),
        ],
        compiler_params=pltpu.CompilerParams(vmem_limit_bytes=VMEM_LIMIT),
        cost_estimate=pl.CostEstimate(
            flops=4 * heads * HD * length * length,
            transcendentals=heads * length * length,
            bytes_accessed=4 * rows * length,
        ),
        name="attend",
    )(qkv, qkv, qkv, seg[None, :], seg[:, None])


def attend_back_kernel(
    heads, nq, block, q_ref, k_ref, v_ref, do_ref, lse_ref, srow_ref, scol_ref, out_ref, dk_ref, dv_ref
):
    h = pl.program_id(0)
    i = pl.program_id(1)
    q = q_ref[...] * jnp.asarray(SCORE_SCALE, BF)
    k = k_ref[...]
    do = do_ref[0]
    s = dot(k, q, 0, 0)
    p = jnp.exp(s - lse_ref[0])
    p = jnp.where(scol_ref[...] == srow_ref[...], p, 0.0)
    dp = dot(v_ref[...], do, 0, 0)
    central = jnp.sum(p * dp, axis=0, keepdims=True)
    ds = (p * (dp - central)).astype(BF)
    dq = dot(k, ds, 1, 0) * SCORE_SCALE
    dk = dot(q, ds, 1, 1)
    dv = dot(do, p.astype(BF), 1, 1)
    out_ref[pl.ds(pl.multiple_of(h * HD, HD), HD), pl.ds(pl.multiple_of(i * block, block), block)] = dq.astype(BF)

    @pl.when(i == 0)
    def _():
        dk_ref[...] = dk
        dv_ref[...] = dv

    @pl.when(i > 0)
    def _():
        dk_ref[...] += dk
        dv_ref[...] += dv

    @pl.when(i == nq - 1)
    def _():
        out_ref[pl.ds(pl.multiple_of((heads + h) * HD, HD), HD), :] = dk_ref[...].astype(BF)
        out_ref[pl.ds(pl.multiple_of((2 * heads + h) * HD, HD), HD), :] = dv_ref[...].astype(BF)


def attend_back(qkv, do, lse, seg, block):
    rows, length = qkv.shape
    heads = rows // (3 * HD)
    nq = length // block
    whole = lambda part: pl.BlockSpec((HD, length), lambda h, i: (part * heads + h, 0))
    return pl.pallas_call(
        functools.partial(attend_back_kernel, heads, nq, block),
        grid=(heads, nq),
        in_specs=[
            pl.BlockSpec((HD, block), lambda h, i: (h, i)),
            whole(1),
            whole(2),
            pl.BlockSpec((1, HD, block), lambda h, i: (i, h, 0)),
            pl.BlockSpec((1, 1, block), lambda h, i: (h, 0, i)),
            pl.BlockSpec((1, block), lambda h, i: (0, i)),
            pl.BlockSpec((length, 1), lambda h, i: (0, 0)),
        ],
        out_specs=pl.BlockSpec((rows, length), lambda h, i: (0, 0)),
        out_shape=jax.ShapeDtypeStruct((rows, length), BF),
        scratch_shapes=[pltpu.VMEM((HD, length), F32), pltpu.VMEM((HD, length), F32)],
        compiler_params=pltpu.CompilerParams(vmem_limit_bytes=VMEM_LIMIT),
        cost_estimate=pl.CostEstimate(
            flops=10 * heads * HD * length * length,
            transcendentals=heads * length * length,
            bytes_accessed=6 * rows * length,
        ),
        name="attend_back",
    )(qkv, qkv, qkv, do, lse, seg[None, :], seg[:, None])


def norm_forward(values_in, gain_vec, bias_vec):
    center = values_in - jnp.mean(values_in, axis=-1, keepdims=True)
    inverse = lax.rsqrt(jnp.mean(center * center, axis=-1, keepdims=True) + EPSILON)
    normed = center * inverse
    return (normed * gain_vec + bias_vec, normed, inverse)


def norm_backward(upstream, normed, inverse, gain_vec):
    scaled = upstream * gain_vec
    inner_sum = (
        scaled
        - jnp.mean(scaled, axis=-1, keepdims=True)
        - normed * jnp.mean(scaled * normed, axis=-1, keepdims=True)
    )
    return (inverse * inner_sum, jnp.sum(upstream * normed, axis=0), jnp.sum(upstream, axis=0))


def segment_ids(lengths, positions):
    starts = jnp.cumsum(lengths) - lengths
    return jnp.sum((positions[:, None] >= starts[None, :]).astype(jnp.int32), axis=1) - 1


def body(
    tokens,
    doc_lengths,
    w_query,
    b_query,
    w_key,
    w_value,
    b_value,
    w_out,
    b_out,
    ln1_gain,
    ln1_bias,
    w_up,
    b_up,
    w_down,
    b_down,
    ln2_gain,
    ln2_bias,
    cotangent,
):
    micro, per_device, ctx_rows, width = tokens.shape
    nc = lax.axis_size("ctx")
    nf = lax.axis_size("fsdp")
    nz = nf // 2
    me = lax.axis_index("ctx")
    fi = lax.axis_index("fsdp")
    core = fi % 2
    rows_w = w_query.shape[0]
    ff_w = w_down.shape[0]
    ff = w_up.shape[1]
    half = ff // 2
    cols = width // nc
    length = ctx_rows * nc
    flat_rows = micro * per_device * ctx_rows
    groups = micro * per_device
    order_a = bits_of(nc)
    order_b = order_a[::-1]

    mine = tokens.reshape(groups, ctx_rows, width)
    inputs_all = [
        gather_ctx(mine[g], order_a if g % 2 == 0 else order_b).reshape(length, width) for g in range(groups)
    ]

    w_qkv = jnp.stack([w_query, w_key, w_value], axis=1).reshape(rows_w, 3, nc, cols)
    w_qkv = exchange_ctx(jnp.moveaxis(w_qkv, 2, 0).reshape(nc, rows_w, 3 * cols))
    w_qkv = gather_z(w_qkv)
    other = core_swap(w_qkv)
    w_qkv = jnp.where(core == 0, jnp.stack([w_qkv, other], axis=2), jnp.stack([other, w_qkv], axis=2))
    w_qkv = jnp.moveaxis(w_qkv.reshape(nz, nc, 2, rows_w, 3 * cols), 0, 1)
    w_qkv = w_qkv.reshape(nc, nz, 2, rows_w, 3 * cols).reshape(width, 3 * cols)

    vectors = (b_query, b_value, b_out, ln1_gain, ln1_bias, b_down, ln2_gain, ln2_bias, b_up)
    packed = jnp.concatenate(vectors)
    packed = lax.all_to_all(
        jnp.broadcast_to(packed[None], (nc * nf,) + packed.shape), BOTH, 0, 0
    ).reshape(nc * nf, packed.shape[0])
    full = [packed[:, j * rows_w : (j + 1) * rows_w].reshape(width) for j in range(8)]
    query_bias, value_bias, out_bias, gain_one, bias_one, down_bias, gain_two, bias_two = full
    up_bias = packed[:, 8 * rows_w :].reshape(nc * nz, 2, ff_w)
    up_bias = lax.dynamic_index_in_dim(up_bias, core, 1, False).reshape(half)

    out_mat = gather_ctx(gather_z(w_out), order_a)
    out_other = core_swap(out_mat)
    out_mat = jnp.where(core == 0, jnp.stack([out_mat, out_other], axis=2), jnp.stack([out_other, out_mat], axis=2))
    out_mat = out_mat.reshape(width, width)

    split = w_up.reshape(rows_w, half // ff_w, 2, ff_w)
    keep = lax.dynamic_index_in_dim(split, core, 2, False).reshape(rows_w, half)
    give = lax.dynamic_index_in_dim(split, 1 - core, 2, False).reshape(rows_w, half)
    got = core_swap(give)
    up_mine = jnp.where(core == 0, jnp.stack([keep, got]), jnp.stack([got, keep])).reshape(2 * rows_w, half)
    up_mat = gather_ctx(gather_z(up_mine), order_a).reshape(width, half)
    down_mat = gather_ctx(gather_z(w_down), order_b).reshape(half, width)

    key_pos = jnp.arange(length, dtype=jnp.int32)
    lengths = doc_lengths.reshape(groups, -1)
    zero_bias = jnp.zeros((cols,), BF)
    qkv_bias = jnp.concatenate(
        [
            lax.dynamic_slice_in_dim(query_bias, me * cols, cols),
            zero_bias,
            lax.dynamic_slice_in_dim(value_bias, me * cols, cols),
        ]
    ).astype(F32)[:, None]
    segs, qkvs, lses, mixed = [], [], [], []
    for g in range(groups):
        seg = segment_ids(lengths[g], key_pos)
        qkv = (dot(w_qkv, inputs_all[g], 0, 1) + qkv_bias).astype(BF)
        o, lse = attend(qkv, seg, ctx_rows)
        mixed.append(exchange_ctx(o).reshape(width, ctx_rows))
        segs.append(seg)
        qkvs.append(qkv)
        lses.append(lse)
    mixed = jnp.concatenate(mixed, axis=1)

    inputs = mine.reshape(flat_rows, width).astype(F32)
    attended = dot(mixed, out_mat, 0, 0) + out_bias
    first, normed_one, inverse_one = norm_forward(inputs + attended, gain_one, bias_one)
    first_low = first.astype(BF)
    both_first = jnp.concatenate([first_low, core_swap(first_low)])
    hidden = dot(both_first, up_mat, 1, 0) + up_bias
    cdf = 0.5 * (1.0 + lax.erf(hidden * 0.7071067811865476))
    slope = (cdf + hidden * jnp.exp(-0.5 * hidden * hidden) * 0.3989422804014327).astype(BF)
    activated = (hidden * cdf).astype(BF)
    part = dot(activated, down_mat, 1, 0)
    branch = part[:flat_rows] + core_swap(part[flat_rows:]) + down_bias
    result, normed_two, inverse_two = norm_forward(first + branch, gain_two, bias_two)
    output = result.astype(BF).reshape(micro, per_device, ctx_rows, width)

    upstream = cotangent.reshape(flat_rows, width).astype(F32)
    grad_h2, grad_gain_two, grad_bias_two = norm_backward(upstream, normed_two, inverse_two, gain_two)
    grad_branch = grad_h2.astype(BF)
    grad_down_bias = jnp.sum(grad_branch.astype(F32), axis=0)
    both_branch = jnp.concatenate([grad_branch, core_swap(grad_branch)])
    grad_down = dot(activated, both_branch, 0, 0).astype(BF).reshape(nc, nz, ff_w, width)
    grad_down = scatter_z(scatter_ctx(grad_down, order_a))
    grad_hidden = (dot(both_branch, down_mat, 1, 1) * slope.astype(F32)).astype(BF)
    grad_up_bias = jnp.sum(grad_hidden.astype(F32), axis=0)
    grad_up = dot(both_first, grad_hidden, 0, 0).astype(BF).reshape(nc, nz, 2, rows_w, half)
    grad_up = scatter_z(scatter_ctx(grad_up, order_b))
    grad_up_mine = lax.dynamic_index_in_dim(grad_up, core, 0, False)
    grad_up_got = core_swap(lax.dynamic_index_in_dim(grad_up, 1 - core, 0, False))
    pair = [t.reshape(rows_w, half // ff_w, ff_w) for t in (grad_up_mine, grad_up_got)]
    grad_up = jnp.where(core == 0, jnp.stack(pair, axis=2), jnp.stack(pair[::-1], axis=2)).reshape(rows_w, ff)
    part = dot(grad_hidden, up_mat, 1, 1)
    grad_first = part[:flat_rows] + core_swap(part[flat_rows:]) + grad_h2
    grad_h1, grad_gain_one, grad_bias_one = norm_backward(grad_first, normed_one, inverse_one, gain_one)
    grad_attended = grad_h1.astype(BF)
    grad_out_bias = jnp.sum(grad_attended.astype(F32), axis=0)
    grad_mixed = dot(out_mat, grad_attended, 1, 1).astype(BF)
    grad_mixed = grad_mixed.reshape(nc, cols, groups, ctx_rows)
    grad_out = dot(mixed, grad_attended, 1, 0).astype(BF).reshape(nc, nz, 2, rows_w, width)
    grad_out_got = core_swap(lax.dynamic_index_in_dim(grad_out, 1 - core, 2, False))
    grad_out = lax.dynamic_index_in_dim(grad_out, core, 2, False).astype(F32) + grad_out_got.astype(F32)
    grad_out = scatter_z(scatter_ctx(grad_out.astype(BF), order_a))

    grad_qkv = None
    grad_bias_parts = []
    input_grads = []
    for g in range(groups):
        do = exchange_ctx(grad_mixed[:, :, g])
        dqkv = attend_back(qkvs[g], do, lses[g], segs[g], ctx_rows)
        grad_bias_parts.append(jnp.sum(dqkv.astype(F32), axis=1))
        now = dot(inputs_all[g], dqkv, 0, 1)
        grad_qkv = now if grad_qkv is None else grad_qkv + now
        back = dot(dqkv, w_qkv, 0, 1).astype(BF).reshape(nc, ctx_rows, width)
        input_grads.append(scatter_ctx(back, order_a if g % 2 == 0 else order_b))
    grad_tokens = grad_h1.reshape(groups, ctx_rows, width) + jnp.stack(input_grads)
    grad_tokens = grad_tokens.reshape(micro, per_device, ctx_rows, width)

    grad_qkv = grad_qkv.astype(BF).reshape(nc, nz, 2, rows_w, 3 * cols)
    grad_qkv_got = core_swap(lax.dynamic_index_in_dim(grad_qkv, 1 - core, 2, False))
    grad_qkv = lax.dynamic_index_in_dim(grad_qkv, core, 2, False).astype(F32) + grad_qkv_got.astype(F32)
    grad_qkv = scatter_z(jnp.moveaxis(grad_qkv.astype(BF), 1, 0))
    grad_qkv = exchange_ctx(grad_qkv).reshape(nc, rows_w, 3, cols)
    grad_qkv = jnp.moveaxis(grad_qkv, 0, 2).reshape(rows_w, 3, width)

    grad_bias = sum(grad_bias_parts).reshape(3, cols)
    spread = lambda v: lax.dynamic_update_slice_in_dim(jnp.zeros((width,), F32), v, me * cols, 0)
    small = [
        spread(grad_bias[0]),
        spread(grad_bias[2]),
        grad_out_bias,
        grad_gain_one,
        grad_bias_one,
        grad_down_bias,
        grad_gain_two,
        grad_bias_two,
    ]
    small = [t.reshape(nc * nf, rows_w) for t in small]
    grad_up_bias = grad_up_bias.reshape(nc * nz, ff_w)
    pair = [jnp.where(core == j, grad_up_bias, 0.0) for j in range(2)]
    small.append(jnp.stack(pair, axis=1).reshape(nc * nf, ff_w))
    small = jnp.concatenate(small, axis=1)
    small = jnp.sum(lax.all_to_all(small, BOTH, 0, 0), axis=0)
    small_out = [small[j * rows_w : (j + 1) * rows_w] for j in range(8)]
    g_bq, g_bv, g_bo, g_g1, g_b1, g_bd, g_g2, g_b2 = small_out
    g_bu = small[8 * rows_w :]

    return (
        output,
        grad_tokens,
        grad_qkv[:, 0],
        g_bq,
        grad_qkv[:, 1],
        grad_qkv[:, 2],
        g_bv,
        grad_out,
        g_bo,
        g_g1,
        g_b1,
        grad_up,
        g_bu,
        grad_down,
        g_bd,
        g_g2,
        g_b2,
    )


def solution(mesh):
    stream = P(None, "fsdp", "ctx", None)
    mat = P(BOTH, None)
    vec = P(BOTH)
    return jax.shard_map(
        body,
        mesh=mesh,
        in_specs=(
            stream,
            P(None, "fsdp", None),
            mat,
            vec,
            mat,
            mat,
            vec,
            mat,
            vec,
            vec,
            vec,
            mat,
            vec,
            mat,
            vec,
            vec,
            vec,
            stream,
        ),
        out_specs=(
            stream,
            stream,
            mat,
            vec,
            mat,
            mat,
            vec,
            mat,
            vec,
            vec,
            vec,
            mat,
            vec,
            mat,
            vec,
            vec,
            vec,
        ),
        check_vma=False,
    )
```

```python
import functools

import jax
import jax.numpy as jnp
from jax import lax
from jax.experimental import pallas as pl
from jax.experimental.pallas import tpu as pltpu
from jax.sharding import PartitionSpec as P

H = 16
HD = 64
EPSILON = 1e-12
SCORE_SCALE = 0.125
MASKED = -1e30
BF = jnp.bfloat16
F32 = jnp.float32
BOTH = ("ctx", "fsdp")
VMEM_LIMIT = 48 << 20


def dot(a, b, ca, cb):
    return lax.dot_general(a, b, (((ca,), (cb,)), ((), ())), preferred_element_type=F32)


def swap(x, axis, r):
    n = lax.axis_size(axis)
    return lax.ppermute(x, axis, [(i, i ^ r) for i in range(n)])


def core_swap(x):
    return swap(x, "fsdp", 1)


def after(x, *first):
    return lax.optimization_barrier((x, first))[0]


def bits_of(n):
    return [1 << b for b in range(n.bit_length() - 1)]


def in_order(mine, got, bit, dim):
    return jnp.where(bit == 0, jnp.stack([mine, got], axis=dim), jnp.stack([got, mine], axis=dim))


def core_groups():
    n = lax.axis_size("fsdp") * lax.axis_size("ctx")
    return [list(range(k, n, 2)) for k in range(2)]


def place(pieces, me):
    n = len(pieces)
    out = jnp.zeros((n,) + pieces[0].shape, pieces[0].dtype)
    for r in range(n):
        out = lax.dynamic_update_index_in_dim(out, pieces[r], me ^ r, 0)
    return out


def pick(x, i):
    return lax.dynamic_index_in_dim(x, i, 0, False)


def gather_z(x):
    n = lax.axis_size("fsdp") // 2
    return [x] + [swap(x, "fsdp", 2 * r) for r in range(1, n)]


def gather_ctx(x, order):
    pieces = {0: x}
    for b in order:
        for r in list(pieces):
            pieces[r ^ b] = swap(pieces[r], "ctx", b)
    return [pieces[r] for r in range(len(pieces))]


def exchange_ctx(x):
    return lax.all_to_all(x, "ctx", 0, 0)


def send_ctx(chunks):
    return [chunks[0]] + [swap(c, "ctx", r) for r, c in enumerate(chunks) if r]


def total_of(pieces):
    out = pieces[0].astype(F32)
    for p in pieces[1:]:
        out = out + p.astype(F32)
    return out


def add_up(x):
    return jnp.sum(x.astype(F32), axis=0).astype(BF)


def z_send(x):
    n = lax.axis_size("fsdp") // 2
    z = lax.axis_index("fsdp") // 2
    return [swap(lax.dynamic_index_in_dim(x, z ^ r, 0, False), "fsdp", 2 * r) for r in range(1, n)]


def z_sum(x, got):
    total = lax.dynamic_index_in_dim(x, lax.axis_index("fsdp") // 2, 0, False).astype(F32)
    for g in got:
        total = total + g.astype(F32)
    return total


def exchange_ctx(x):
    return lax.all_to_all(x, "ctx", 0, 0)


def attend_kernel(q_ref, k_ref, v_ref, srow_ref, scol_ref, o_ref, lse_ref):
    q = q_ref[...] * jnp.asarray(SCORE_SCALE, BF)
    s = dot(k_ref[...], q, 0, 0)
    s = jnp.where(scol_ref[...] == srow_ref[...], s, MASKED)
    top = jnp.max(s, axis=0, keepdims=True)
    p = jnp.exp(s - top)
    total = jnp.sum(p, axis=0, keepdims=True)
    o = dot(v_ref[...], p.astype(BF), 1, 0)
    o_ref[...] = (o / total).astype(BF)[None]
    lse_ref[...] = (top + jnp.log(total))[None]


def attend(qkv, seg, block):
    rows, length = qkv.shape
    heads = rows // (3 * HD)
    nq = length // block
    whole = lambda part: pl.BlockSpec((HD, length), lambda h, i: (part * heads + h, 0))
    return pl.pallas_call(
        attend_kernel,
        grid=(heads, nq),
        in_specs=[
            pl.BlockSpec((HD, block), lambda h, i: (h, i)),
            whole(1),
            whole(2),
            pl.BlockSpec((1, block), lambda h, i: (0, i)),
            pl.BlockSpec((length, 1), lambda h, i: (0, 0)),
        ],
        out_specs=[
            pl.BlockSpec((1, HD, block), lambda h, i: (i, h, 0)),
            pl.BlockSpec((1, 1, block), lambda h, i: (h, 0, i)),
        ],
        out_shape=[
            jax.ShapeDtypeStruct((nq, heads * HD, block), BF),
            jax.ShapeDtypeStruct((heads, 1, length), F32),
        ],
        compiler_params=pltpu.CompilerParams(vmem_limit_bytes=VMEM_LIMIT),
        cost_estimate=pl.CostEstimate(
            flops=1 << 20,
            transcendentals=1 << 10,
            bytes_accessed=1 << 20,
        ),
        name="attend",
    )(qkv, qkv, qkv, seg[None, :], seg[:, None])


def attend_back_kernel(
    heads, nq, block, q_ref, k_ref, v_ref, do_ref, lse_ref, srow_ref, scol_ref, out_ref, dk_ref, dv_ref
):
    h = pl.program_id(0)
    i = pl.program_id(1)
    q = q_ref[...] * jnp.asarray(SCORE_SCALE, BF)
    k = k_ref[...]
    do = do_ref[0]
    s = dot(k, q, 0, 0)
    p = jnp.exp(s - lse_ref[0])
    p = jnp.where(scol_ref[...] == srow_ref[...], p, 0.0)
    dp = dot(v_ref[...], do, 0, 0)
    central = jnp.sum(p * dp, axis=0, keepdims=True)
    ds = (p * (dp - central)).astype(BF)
    dq = dot(k, ds, 1, 0) * SCORE_SCALE
    dk = dot(q, ds, 1, 1)
    dv = dot(do, p.astype(BF), 1, 1)
    out_ref[pl.ds(pl.multiple_of(h * HD, HD), HD), pl.ds(pl.multiple_of(i * block, block), block)] = dq.astype(BF)

    @pl.when(i == 0)
    def _():
        dk_ref[...] = dk
        dv_ref[...] = dv

    @pl.when(i > 0)
    def _():
        dk_ref[...] += dk
        dv_ref[...] += dv

    @pl.when(i == nq - 1)
    def _():
        out_ref[pl.ds(pl.multiple_of((heads + h) * HD, HD), HD), :] = dk_ref[...].astype(BF)
        out_ref[pl.ds(pl.multiple_of((2 * heads + h) * HD, HD), HD), :] = dv_ref[...].astype(BF)


def attend_back(qkv, do, group, lse, seg, block):
    rows, length = qkv.shape
    heads = rows // (3 * HD)
    nq = length // block
    whole = lambda part: pl.BlockSpec((HD, length), lambda h, i: (part * heads + h, 0))
    return pl.pallas_call(
        functools.partial(attend_back_kernel, heads, nq, block),
        grid=(heads, nq),
        in_specs=[
            pl.BlockSpec((HD, block), lambda h, i: (h, i)),
            whole(1),
            whole(2),
            pl.BlockSpec((1, HD, block), lambda h, i: (i, h, group)),
            pl.BlockSpec((1, 1, block), lambda h, i: (h, 0, i)),
            pl.BlockSpec((1, block), lambda h, i: (0, i)),
            pl.BlockSpec((length, 1), lambda h, i: (0, 0)),
        ],
        out_specs=pl.BlockSpec((rows, length), lambda h, i: (0, 0)),
        out_shape=jax.ShapeDtypeStruct((rows, length), BF),
        scratch_shapes=[pltpu.VMEM((HD, length), F32), pltpu.VMEM((HD, length), F32)],
        compiler_params=pltpu.CompilerParams(vmem_limit_bytes=VMEM_LIMIT),
        cost_estimate=pl.CostEstimate(
            flops=1 << 20,
            transcendentals=1 << 10,
            bytes_accessed=1 << 20,
        ),
        name="attend_back",
    )(qkv, qkv, qkv, do, lse, seg[None, :], seg[:, None])


def norm_forward(values_in, gain_vec, bias_vec):
    center = values_in - jnp.mean(values_in, axis=-1, keepdims=True)
    inverse = lax.rsqrt(jnp.mean(center * center, axis=-1, keepdims=True) + EPSILON)
    normed = center * inverse
    return (normed * gain_vec + bias_vec, normed, inverse)


def norm_backward(upstream, normed, inverse, gain_vec):
    scaled = upstream * gain_vec
    inner_sum = (
        scaled
        - jnp.mean(scaled, axis=-1, keepdims=True)
        - normed * jnp.mean(scaled * normed, axis=-1, keepdims=True)
    )
    return (inverse * inner_sum, jnp.sum(upstream * normed, axis=0), jnp.sum(upstream, axis=0))


def segment_ids(lengths, positions):
    starts = jnp.cumsum(lengths) - lengths
    return jnp.sum((positions[:, None] >= starts[None, :]).astype(jnp.int32), axis=1) - 1


def body(
    tokens,
    doc_lengths,
    w_query,
    b_query,
    w_key,
    w_value,
    b_value,
    w_out,
    b_out,
    ln1_gain,
    ln1_bias,
    w_up,
    b_up,
    w_down,
    b_down,
    ln2_gain,
    ln2_bias,
    cotangent,
):
    micro, per_device, ctx_rows, width = tokens.shape
    nc = lax.axis_size("ctx")
    nf = lax.axis_size("fsdp")
    nz = nf // 2
    me = lax.axis_index("ctx")
    fi = lax.axis_index("fsdp")
    core = fi % 2
    rows_w = w_query.shape[0]
    ff_w = w_down.shape[0]
    ff = w_up.shape[1]
    half = ff // 2
    cols = width // nc
    length = ctx_rows * nc
    flat_rows = micro * per_device * ctx_rows
    groups = micro * per_device
    order_a = bits_of(nc)
    order_b = order_a[::-1]
    me_c, me_z = me, fi // 2

    w_qkv = jnp.stack([w_query, w_key, w_value], axis=1).reshape(rows_w, 3, nc, cols)
    w_qkv = jnp.moveaxis(w_qkv, 2, 0).reshape(nc, rows_w, 3 * cols)
    vectors = (b_query, b_value, b_out, ln1_gain, ln1_bias, b_down, ln2_gain, ln2_bias, b_up)
    packed = jnp.concatenate(vectors)
    packed = jnp.pad(packed, (0, 8 * 3 * cols - packed.shape[0])).reshape(1, 8, 3 * cols)
    sent = jnp.concatenate([w_qkv, jnp.broadcast_to(packed, (nc, 8, 3 * cols))], axis=1)
    sent_c = send_ctx([pick(sent, me ^ r) for r in range(nc)])
    sent_z = gather_z(place(sent_c, me_c))
    mine = tokens.reshape(groups, ctx_rows, width)
    inputs_all = []
    for g in range(groups):
        rows_now = after(mine[g], sent_c) if g == 0 else after(mine[g], inputs_all[g - 1])
        inputs_all.append(exchange_ctx(jnp.broadcast_to(rows_now[None], (nc, ctx_rows, width))))
    inputs_all = [t.reshape(length, width) for t in inputs_all]
    sent = place(sent_z, me_z)
    sent = in_order(sent, core_swap(sent), core, 2)
    sent = jnp.moveaxis(sent, 0, 1)
    w_qkv = sent[:, :, :, :rows_w].reshape(width, 3 * cols)
    packed = sent[:, :, :, rows_w:].reshape(nc * nf, 8 * 3 * cols)
    full = [packed[:, j * rows_w : (j + 1) * rows_w].reshape(width) for j in range(8)]
    query_bias, value_bias, out_bias, gain_one, bias_one, down_bias, gain_two, bias_two = full
    up_bias = packed[:, 8 * rows_w : 8 * rows_w + ff_w].reshape(nc * nz, 2, ff_w)
    up_bias = lax.dynamic_index_in_dim(up_bias, core, 1, False).reshape(half)

    split = w_up.reshape(rows_w, half // ff_w, 2, ff_w)
    keep = lax.dynamic_index_in_dim(split, core, 2, False).reshape(rows_w, half)
    give = lax.dynamic_index_in_dim(split, 1 - core, 2, False).reshape(rows_w, half)
    up_mine = in_order(keep, core_swap(give), core, 0).reshape(2 * rows_w, half)
    parts = half // width
    own = jnp.concatenate([up_mine[:, j * width : (j + 1) * width] for j in range(parts)] + [w_down, w_out])
    own = lax.all_gather(own, BOTH, axis=0, axis_index_groups=core_groups())

    key_pos = jnp.arange(length, dtype=jnp.int32)
    lengths = doc_lengths.reshape(groups, -1)
    zero_bias = jnp.zeros((cols,), BF)
    qkv_bias = jnp.concatenate(
        [
            lax.dynamic_slice_in_dim(query_bias, me * cols, cols),
            zero_bias,
            lax.dynamic_slice_in_dim(value_bias, me * cols, cols),
        ]
    ).astype(F32)[:, None]
    segs, qkvs, lses, mixed = [], [], [], []
    outs = []
    for g in range(groups):
        segs.append(segment_ids(lengths[g], key_pos))
        rows_now = inputs_all[g] if g == 0 else after(inputs_all[g], outs[0])
        qkvs.append((dot(w_qkv, rows_now, 0, 1) + qkv_bias).astype(BF))
        o, lse = attend(qkvs[g], segs[g], ctx_rows)
        outs.append(o)
        lses.append(lse)
        mixed.append(exchange_ctx(o if g == 0 else after(o, mixed[-1])))
    own = after(own, mixed[-1])
    mixed = jnp.concatenate([t.reshape(width, ctx_rows) for t in mixed], axis=1)
    n_up = 2 * rows_w * parts
    up_mat = jnp.concatenate(
        [own[:, j * 2 * rows_w : (j + 1) * 2 * rows_w].reshape(width, width) for j in range(parts)], axis=1
    )
    down_mat = own[:, n_up : n_up + ff_w].reshape(half, width)
    out_mine = own[:, n_up + ff_w :]
    out_mat = in_order(out_mine, core_swap(out_mine), core, 1).reshape(width, width)

    inputs = mine.reshape(flat_rows, width).astype(F32)
    attended = dot(mixed, out_mat, 0, 0) + out_bias
    first, normed_one, inverse_one = norm_forward(inputs + attended, gain_one, bias_one)
    first_low = first.astype(BF)
    both_first = jnp.concatenate([first_low, core_swap(first_low)])
    hidden = dot(both_first, up_mat, 1, 0) + up_bias
    cdf = 0.5 * (1.0 + lax.erf(hidden * 0.7071067811865476))
    slope = (cdf + hidden * jnp.exp(-0.5 * hidden * hidden) * 0.3989422804014327).astype(BF)
    activated = (hidden * cdf).astype(BF)
    part = dot(activated, down_mat, 1, 0)
    branch = part[:flat_rows] + core_swap(part[flat_rows:]) + down_bias
    result, normed_two, inverse_two = norm_forward(first + branch, gain_two, bias_two)
    output = result.astype(BF).reshape(micro, per_device, ctx_rows, width)

    upstream = cotangent.reshape(flat_rows, width).astype(F32)
    grad_h2, grad_gain_two, grad_bias_two = norm_backward(upstream, normed_two, inverse_two, gain_two)
    grad_branch = grad_h2.astype(BF)
    grad_down_bias = jnp.sum(grad_branch.astype(F32), axis=0)
    both_branch = jnp.concatenate([grad_branch, core_swap(grad_branch)])
    grad_down = dot(activated, both_branch, 0, 0).astype(BF)
    grad_hidden = (dot(both_branch, down_mat, 1, 1) * slope.astype(F32)).astype(BF)
    grad_up_bias = jnp.sum(grad_hidden.astype(F32), axis=0)
    grad_ups = [
        dot(both_first, grad_hidden[:, j * width : (j + 1) * width], 0, 0).astype(BF) for j in range(parts)
    ]
    grad_ffn = jnp.concatenate(
        [t.reshape(nc * nz, 2 * rows_w, width) for t in grad_ups] + [grad_down.reshape(nc * nz, ff_w, width)], axis=1
    )
    grad_ffn = lax.psum_scatter(grad_ffn, BOTH, scatter_dimension=0, axis_index_groups=core_groups()).astype(F32)
    grad_down = grad_ffn[n_up:]
    part = dot(grad_hidden, up_mat, 1, 1)
    grad_first = part[:flat_rows] + core_swap(part[flat_rows:]) + grad_h2
    grad_h1, grad_gain_one, grad_bias_one = norm_backward(grad_first, normed_one, inverse_one, gain_one)
    grad_attended = grad_h1.astype(BF)
    grad_out_bias = jnp.sum(grad_attended.astype(F32), axis=0)
    grad_mixed = dot(out_mat, grad_attended, 1, 1).astype(BF)
    grad_mixed = grad_mixed.reshape(nc, cols, groups, ctx_rows)
    dos = []
    for g in range(groups):
        do = grad_mixed[:, :, g]
        dos.append(exchange_ctx(do if g == 0 else after(do, dos[0])))
    grad_out = dot(mixed, grad_attended, 1, 0).astype(BF).reshape(nc, nz, 2, rows_w, width)
    grad_out_got = core_swap(lax.dynamic_index_in_dim(grad_out, 1 - core, 2, False))
    grad_out = lax.dynamic_index_in_dim(grad_out, core, 2, False).astype(F32) + grad_out_got.astype(F32)
    grad_out = after(grad_out.astype(BF), dos[0])
    out_raw = send_ctx([pick(grad_out, me ^ r) for r in range(nc)])

    backs = []
    grad_qkv = None
    grad_bias_parts = []
    for g in range(groups):
        dqkv = attend_back(qkvs[g], dos[g], 0, lses[g], segs[g], ctx_rows)
        if g == 1:
            dqkv, backs[0] = lax.optimization_barrier((dqkv, backs[0]))
        grad_bias_parts.append(jnp.sum(dqkv.astype(F32), axis=1))
        back = dot(dqkv, w_qkv, 0, 1).astype(BF).reshape(nc, ctx_rows, width)
        if g + 1 < groups:
            qkvs[g + 1] = after(qkvs[g + 1], back)
        backs.append(exchange_ctx(back))
        now = dot(inputs_all[g], dqkv, 0, 1)
        grad_qkv = now if grad_qkv is None else grad_qkv + now
    grad_bias = sum(grad_bias_parts).reshape(3, cols)
    spread = lambda v: lax.dynamic_update_slice_in_dim(jnp.zeros((width,), F32), v, me * cols, 0)
    small = [
        spread(grad_bias[0]),
        spread(grad_bias[2]),
        grad_out_bias,
        grad_gain_one,
        grad_bias_one,
        grad_down_bias,
        grad_gain_two,
        grad_bias_two,
    ]
    small = [t.reshape(nc * nf, rows_w) for t in small]
    grad_up_bias = grad_up_bias.reshape(nc * nz, ff_w)
    pair = [jnp.where(core == j, grad_up_bias, 0.0) for j in range(2)]
    small.append(jnp.stack(pair, axis=1).reshape(nc * nf, ff_w))
    small = jnp.concatenate(small, axis=1)
    grad_qkv = grad_qkv.astype(BF).reshape(nc, nz, 2, rows_w, 3 * cols)
    grad_qkv_got = core_swap(lax.dynamic_index_in_dim(grad_qkv, 1 - core, 2, False))
    grad_out = total_of(after(out_raw, dqkv)).astype(BF)
    out_got = z_send(grad_out)
    grad_qkv = lax.dynamic_index_in_dim(grad_qkv, core, 2, False).astype(F32) + grad_qkv_got.astype(F32)
    grad_qkv = jnp.moveaxis(grad_qkv.astype(BF), 1, 0)
    grad_qkv = z_sum(grad_qkv, z_send(grad_qkv))
    small = jnp.sum(lax.all_to_all(after(small, backs[-1]), BOTH, 0, 0), axis=0)
    grad_qkv = exchange_ctx(after(grad_qkv, backs[-1])).reshape(nc, rows_w, 3, cols)
    grad_qkv = jnp.moveaxis(grad_qkv, 0, 2).reshape(rows_w, 3, width)
    input_grads = [jnp.sum(t.astype(F32), axis=0) for t in backs]
    grad_out = z_sum(grad_out, out_got)
    grad_up = [grad_ffn[j * 2 * rows_w : (j + 1) * 2 * rows_w] for j in range(parts)]
    grad_up = jnp.concatenate(grad_up, axis=1).reshape(2, rows_w, half)
    grad_up_got = core_swap(lax.dynamic_index_in_dim(grad_up, 1 - core, 0, False))
    pair = [
        t.reshape(rows_w, half // ff_w, ff_w)
        for t in (lax.dynamic_index_in_dim(grad_up, core, 0, False), grad_up_got)
    ]
    grad_up = in_order(pair[0], pair[1], core, 2).reshape(rows_w, ff)
    grad_tokens = grad_h1.reshape(groups, ctx_rows, width) + jnp.stack(input_grads)
    grad_tokens = grad_tokens.reshape(micro, per_device, ctx_rows, width)

    small_out = [small[j * rows_w : (j + 1) * rows_w] for j in range(8)]
    g_bq, g_bv, g_bo, g_g1, g_b1, g_bd, g_g2, g_b2 = small_out
    g_bu = small[8 * rows_w :]

    return (
        output,
        grad_tokens,
        grad_qkv[:, 0],
        g_bq,
        grad_qkv[:, 1],
        grad_qkv[:, 2],
        g_bv,
        grad_out,
        g_bo,
        g_g1,
        g_b1,
        grad_up,
        g_bu,
        grad_down,
        g_bd,
        g_g2,
        g_b2,
    )


def solution(mesh):
    stream = P(None, "fsdp", "ctx", None)
    mat = P(BOTH, None)
    vec = P(BOTH)
    return jax.shard_map(
        body,
        mesh=mesh,
        in_specs=(
            stream,
            P(None, "fsdp", None),
            mat,
            vec,
            mat,
            mat,
            vec,
            mat,
            vec,
            vec,
            vec,
            mat,
            vec,
            mat,
            vec,
            vec,
            vec,
            stream,
        ),
        out_specs=(
            stream,
            stream,
            mat,
            vec,
            mat,
            mat,
            vec,
            mat,
            vec,
            vec,
            vec,
            mat,
            vec,
            mat,
            vec,
            vec,
            vec,
        ),
        check_vma=False,
    )
```

```python
import functools

import jax
import jax.numpy as jnp
from jax import lax
from jax.experimental import pallas as pl
from jax.experimental.pallas import tpu as pltpu
from jax.sharding import PartitionSpec as P

H = 16
HD = 64
EPSILON = 1e-12
SCORE_SCALE = 0.125
MASKED = -1e30
BF = jnp.bfloat16
F32 = jnp.float32
BOTH = ("ctx", "fsdp")
VMEM_LIMIT = 48 << 20


def dot(a, b, ca, cb):
    return lax.dot_general(a, b, (((ca,), (cb,)), ((), ())), preferred_element_type=F32)


def swap(x, axis, r):
    n = lax.axis_size(axis)
    return lax.ppermute(x, axis, [(i, i ^ r) for i in range(n)])


def core_swap(x):
    return swap(x, "fsdp", 1)


def after(x, *first):
    return lax.optimization_barrier((x, first))[0]


def bits_of(n):
    return [1 << b for b in range(n.bit_length() - 1)]


def in_order(mine, got, bit, dim):
    return jnp.where(bit == 0, jnp.stack([mine, got], axis=dim), jnp.stack([got, mine], axis=dim))


def core_groups():
    n = lax.axis_size("fsdp") * lax.axis_size("ctx")
    return [list(range(k, n, 2)) for k in range(2)]


def z_groups():
    n = lax.axis_size("fsdp")
    return [list(range(k, n, 2)) for k in range(2)]


def place(pieces, me):
    n = len(pieces)
    out = jnp.zeros((n,) + pieces[0].shape, pieces[0].dtype)
    for r in range(n):
        out = lax.dynamic_update_index_in_dim(out, pieces[r], me ^ r, 0)
    return out


def pick(x, i):
    return lax.dynamic_index_in_dim(x, i, 0, False)


def gather_z(x):
    n = lax.axis_size("fsdp") // 2
    return [x] + [swap(x, "fsdp", 2 * r) for r in range(1, n)]


def gather_ctx(x, order):
    pieces = {0: x}
    for b in order:
        for r in list(pieces):
            pieces[r ^ b] = swap(pieces[r], "ctx", b)
    return [pieces[r] for r in range(len(pieces))]


def exchange_ctx(x):
    return lax.all_to_all(x, "ctx", 0, 0)


def send_ctx(chunks):
    return [chunks[0]] + [swap(c, "ctx", r) for r, c in enumerate(chunks) if r]


def total_of(pieces):
    out = pieces[0].astype(F32)
    for p in pieces[1:]:
        out = out + p.astype(F32)
    return out


def add_up(x):
    return jnp.sum(x.astype(F32), axis=0).astype(BF)


def z_send(x):
    n = lax.axis_size("fsdp") // 2
    z = lax.axis_index("fsdp") // 2
    return [swap(lax.dynamic_index_in_dim(x, z ^ r, 0, False), "fsdp", 2 * r) for r in range(1, n)]


def z_sum(x, got):
    total = lax.dynamic_index_in_dim(x, lax.axis_index("fsdp") // 2, 0, False).astype(F32)
    for g in got:
        total = total + g.astype(F32)
    return total


def exchange_ctx(x):
    return lax.all_to_all(x, "ctx", 0, 0)


def attend_kernel(q_ref, k_ref, v_ref, srow_ref, scol_ref, o_ref, lse_ref):
    q = q_ref[...] * jnp.asarray(SCORE_SCALE, BF)
    s = dot(k_ref[...], q, 0, 0)
    s = jnp.where(scol_ref[...] == srow_ref[...], s, MASKED)
    top = jnp.max(s, axis=0, keepdims=True)
    p = jnp.exp(s - top)
    total = jnp.sum(p, axis=0, keepdims=True)
    o = dot(v_ref[...], p.astype(BF), 1, 0)
    o_ref[...] = (o / total).astype(BF)[None]
    lse_ref[...] = (top + jnp.log(total))[None]


def attend(qkv, seg, block):
    rows, length = qkv.shape
    heads = rows // (3 * HD)
    nq = length // block
    whole = lambda part: pl.BlockSpec((HD, length), lambda h, i: (part * heads + h, 0))
    return pl.pallas_call(
        attend_kernel,
        grid=(heads, nq),
        in_specs=[
            pl.BlockSpec((HD, block), lambda h, i: (h, i)),
            whole(1),
            whole(2),
            pl.BlockSpec((1, block), lambda h, i: (0, i)),
            pl.BlockSpec((length, 1), lambda h, i: (0, 0)),
        ],
        out_specs=[
            pl.BlockSpec((1, HD, block), lambda h, i: (i, h, 0)),
            pl.BlockSpec((1, 1, block), lambda h, i: (h, 0, i)),
        ],
        out_shape=[
            jax.ShapeDtypeStruct((nq, heads * HD, block), BF),
            jax.ShapeDtypeStruct((heads, 1, length), F32),
        ],
        compiler_params=pltpu.CompilerParams(vmem_limit_bytes=VMEM_LIMIT),
        cost_estimate=pl.CostEstimate(
            flops=1 << 20,
            transcendentals=1 << 10,
            bytes_accessed=1 << 20,
        ),
        name="attend",
    )(qkv, qkv, qkv, seg[None, :], seg[:, None])


def attend_back_kernel(
    heads, nq, block, q_ref, k_ref, v_ref, do_ref, lse_ref, srow_ref, scol_ref, out_ref, dk_ref, dv_ref
):
    h = pl.program_id(0)
    i = pl.program_id(1)
    q = q_ref[...] * jnp.asarray(SCORE_SCALE, BF)
    k = k_ref[...]
    do = do_ref[0]
    s = dot(k, q, 0, 0)
    p = jnp.exp(s - lse_ref[0])
    p = jnp.where(scol_ref[...] == srow_ref[...], p, 0.0)
    dp = dot(v_ref[...], do, 0, 0)
    central = jnp.sum(p * dp, axis=0, keepdims=True)
    ds = (p * (dp - central)).astype(BF)
    dq = dot(k, ds, 1, 0) * SCORE_SCALE
    dk = dot(q, ds, 1, 1)
    dv = dot(do, p.astype(BF), 1, 1)
    out_ref[pl.ds(pl.multiple_of(h * HD, HD), HD), pl.ds(pl.multiple_of(i * block, block), block)] = dq.astype(BF)

    @pl.when(i == 0)
    def _():
        dk_ref[...] = dk
        dv_ref[...] = dv

    @pl.when(i > 0)
    def _():
        dk_ref[...] += dk
        dv_ref[...] += dv

    @pl.when(i == nq - 1)
    def _():
        out_ref[pl.ds(pl.multiple_of((heads + h) * HD, HD), HD), :] = dk_ref[...].astype(BF)
        out_ref[pl.ds(pl.multiple_of((2 * heads + h) * HD, HD), HD), :] = dv_ref[...].astype(BF)


def attend_back(qkv, do, group, lse, seg, block):
    rows, length = qkv.shape
    heads = rows // (3 * HD)
    nq = length // block
    whole = lambda part: pl.BlockSpec((HD, length), lambda h, i: (part * heads + h, 0))
    return pl.pallas_call(
        functools.partial(attend_back_kernel, heads, nq, block),
        grid=(heads, nq),
        in_specs=[
            pl.BlockSpec((HD, block), lambda h, i: (h, i)),
            whole(1),
            whole(2),
            pl.BlockSpec((1, HD, block), lambda h, i: (i, h, group)),
            pl.BlockSpec((1, 1, block), lambda h, i: (h, 0, i)),
            pl.BlockSpec((1, block), lambda h, i: (0, i)),
            pl.BlockSpec((length, 1), lambda h, i: (0, 0)),
        ],
        out_specs=pl.BlockSpec((rows, length), lambda h, i: (0, 0)),
        out_shape=jax.ShapeDtypeStruct((rows, length), BF),
        scratch_shapes=[pltpu.VMEM((HD, length), F32), pltpu.VMEM((HD, length), F32)],
        compiler_params=pltpu.CompilerParams(vmem_limit_bytes=VMEM_LIMIT),
        cost_estimate=pl.CostEstimate(
            flops=1 << 20,
            transcendentals=1 << 10,
            bytes_accessed=1 << 20,
        ),
        name="attend_back",
    )(qkv, qkv, qkv, do, lse, seg[None, :], seg[:, None])


def norm_forward(values_in, gain_vec, bias_vec):
    center = values_in - jnp.mean(values_in, axis=-1, keepdims=True)
    inverse = lax.rsqrt(jnp.mean(center * center, axis=-1, keepdims=True) + EPSILON)
    normed = center * inverse
    return (normed * gain_vec + bias_vec, normed, inverse)


def norm_backward(upstream, normed, inverse, gain_vec):
    scaled = upstream * gain_vec
    inner_sum = (
        scaled
        - jnp.mean(scaled, axis=-1, keepdims=True)
        - normed * jnp.mean(scaled * normed, axis=-1, keepdims=True)
    )
    return (inverse * inner_sum, jnp.sum(upstream * normed, axis=0), jnp.sum(upstream, axis=0))


def segment_ids(lengths, positions):
    starts = jnp.cumsum(lengths) - lengths
    return jnp.sum((positions[:, None] >= starts[None, :]).astype(jnp.int32), axis=1) - 1


def body(
    tokens,
    doc_lengths,
    w_query,
    b_query,
    w_key,
    w_value,
    b_value,
    w_out,
    b_out,
    ln1_gain,
    ln1_bias,
    w_up,
    b_up,
    w_down,
    b_down,
    ln2_gain,
    ln2_bias,
    cotangent,
):
    micro, per_device, ctx_rows, width = tokens.shape
    nc = lax.axis_size("ctx")
    nf = lax.axis_size("fsdp")
    nz = nf // 2
    me = lax.axis_index("ctx")
    fi = lax.axis_index("fsdp")
    core = fi % 2
    rows_w = w_query.shape[0]
    ff_w = w_down.shape[0]
    ff = w_up.shape[1]
    half = ff // 2
    cols = width // nc
    length = ctx_rows * nc
    flat_rows = micro * per_device * ctx_rows
    groups = micro * per_device
    order_a = bits_of(nc)
    order_b = order_a[::-1]
    me_c, me_z = me, fi // 2

    w_qkv = jnp.stack([w_query, w_key, w_value], axis=1).reshape(rows_w, 3, nc, cols)
    w_qkv = jnp.moveaxis(w_qkv, 2, 0).reshape(nc, rows_w, 3 * cols)
    vectors = (b_query, b_value, b_out, ln1_gain, ln1_bias, b_down, ln2_gain, ln2_bias, b_up)
    packed = jnp.concatenate(vectors)
    packed = jnp.pad(packed, (0, 8 * 3 * cols - packed.shape[0])).reshape(1, 8, 3 * cols)
    sent = jnp.concatenate([w_qkv, jnp.broadcast_to(packed, (nc, 8, 3 * cols))], axis=1)
    sent_c = send_ctx([pick(sent, me ^ r) for r in range(nc)])
    sent_z = gather_z(place(sent_c, me_c))
    mine = tokens.reshape(groups, ctx_rows, width)
    inputs_all = []
    for g in range(groups):
        rows_now = after(mine[g], sent_c) if g == 0 else after(mine[g], inputs_all[g - 1])
        inputs_all.append(exchange_ctx(jnp.broadcast_to(rows_now[None], (nc, ctx_rows, width))))
    inputs_all = [t.reshape(length, width) for t in inputs_all]
    sent = place(sent_z, me_z)
    sent = in_order(sent, core_swap(sent), core, 2)
    sent = jnp.moveaxis(sent, 0, 1)
    w_qkv = sent[:, :, :, :rows_w].reshape(width, 3 * cols)
    packed = sent[:, :, :, rows_w:].reshape(nc * nf, 8 * 3 * cols)
    full = [packed[:, j * rows_w : (j + 1) * rows_w].reshape(width) for j in range(8)]
    query_bias, value_bias, out_bias, gain_one, bias_one, down_bias, gain_two, bias_two = full
    up_bias = packed[:, 8 * rows_w : 8 * rows_w + ff_w].reshape(nc * nz, 2, ff_w)
    up_bias = lax.dynamic_index_in_dim(up_bias, core, 1, False).reshape(half)

    split = w_up.reshape(rows_w, half // ff_w, 2, ff_w)
    keep = lax.dynamic_index_in_dim(split, core, 2, False).reshape(rows_w, half)
    give = lax.dynamic_index_in_dim(split, 1 - core, 2, False).reshape(rows_w, half)
    up_mine = in_order(keep, core_swap(give), core, 0).reshape(2 * rows_w, half)
    parts = half // width
    own = jnp.concatenate([up_mine[:, j * width : (j + 1) * width] for j in range(parts)] + [w_down])
    own = lax.all_gather(own, BOTH, axis=0, axis_index_groups=core_groups())

    key_pos = jnp.arange(length, dtype=jnp.int32)
    lengths = doc_lengths.reshape(groups, -1)
    zero_bias = jnp.zeros((cols,), BF)
    qkv_bias = jnp.concatenate(
        [
            lax.dynamic_slice_in_dim(query_bias, me * cols, cols),
            zero_bias,
            lax.dynamic_slice_in_dim(value_bias, me * cols, cols),
        ]
    ).astype(F32)[:, None]
    segs, qkvs, lses, mixed = [], [], [], []
    outs = []
    for g in range(groups):
        segs.append(segment_ids(lengths[g], key_pos))
        rows_now = inputs_all[g] if g == 0 else after(inputs_all[g], outs[0])
        qkvs.append((dot(w_qkv, rows_now, 0, 1) + qkv_bias).astype(BF))
        o, lse = attend(qkvs[g], segs[g], ctx_rows)
        outs.append(o)
        lses.append(lse)
        mixed.append(exchange_ctx(o if g == 0 else after(o, mixed[-1])))
    out_c = send_ctx([place(gather_z(after(w_out, outs[0])), me_z)] * nc)
    out_mat = place(after(out_c, outs[-1]), me_c)
    out_mat = in_order(out_mat, core_swap(out_mat), core, 2).reshape(width, width)
    own = after(own, mixed[-1])
    mixed = jnp.concatenate([t.reshape(width, ctx_rows) for t in mixed], axis=1)
    n_up = 2 * rows_w * parts
    up_mat = jnp.concatenate(
        [own[:, j * 2 * rows_w : (j + 1) * 2 * rows_w].reshape(width, width) for j in range(parts)], axis=1
    )
    down_mat = own[:, n_up : n_up + ff_w].reshape(half, width)
    inputs = mine.reshape(flat_rows, width).astype(F32)
    attended = dot(mixed, out_mat, 0, 0) + out_bias
    first, normed_one, inverse_one = norm_forward(inputs + attended, gain_one, bias_one)
    first_low = first.astype(BF)
    both_first = jnp.concatenate([first_low, core_swap(first_low)])
    hidden = dot(both_first, up_mat, 1, 0) + up_bias
    cdf = 0.5 * (1.0 + lax.erf(hidden * 0.7071067811865476))
    slope = (cdf + hidden * jnp.exp(-0.5 * hidden * hidden) * 0.3989422804014327).astype(BF)
    activated = (hidden * cdf).astype(BF)
    away = core_swap(dot(activated[flat_rows:], down_mat, 1, 0).astype(BF))
    branch = dot(activated[:flat_rows], down_mat, 1, 0) + away.astype(F32) + down_bias
    result, normed_two, inverse_two = norm_forward(first + branch, gain_two, bias_two)
    output = result.astype(BF).reshape(micro, per_device, ctx_rows, width)

    upstream = cotangent.reshape(flat_rows, width).astype(F32)
    grad_h2, grad_gain_two, grad_bias_two = norm_backward(upstream, normed_two, inverse_two, gain_two)
    grad_branch = grad_h2.astype(BF)
    grad_down_bias = jnp.sum(grad_branch.astype(F32), axis=0)
    both_branch = jnp.concatenate([grad_branch, core_swap(grad_branch)])
    grad_down = dot(activated, both_branch, 0, 0).astype(BF)
    both_branch = lax.optimization_barrier((both_branch, grad_down))[0]
    grad_down = lax.psum_scatter(grad_down, "ctx", scatter_dimension=0, tiled=True)
    grad_hidden = (dot(both_branch, down_mat, 1, 1) * slope.astype(F32)).astype(BF)
    grad_up_bias = dot(jnp.ones((8, grad_hidden.shape[0]), BF), grad_hidden, 1, 0)[0]
    grad_ups = [
        dot(both_first, grad_hidden[:, j * width : (j + 1) * width], 0, 0).astype(BF) for j in range(parts)
    ]
    away = core_swap(dot(grad_hidden[flat_rows:], up_mat, 1, 1).astype(BF))
    grad_first = dot(grad_hidden[:flat_rows], up_mat, 1, 1) + away.astype(F32) + grad_h2
    grad_h1, grad_gain_one, grad_bias_one = norm_backward(grad_first, normed_one, inverse_one, gain_one)
    grad_attended = grad_h1.astype(BF)
    grad_out_bias = jnp.sum(grad_attended.astype(F32), axis=0)
    dos = []
    for g in range(groups):
        do = dot(out_mat, grad_attended[g * ctx_rows : (g + 1) * ctx_rows], 1, 1).astype(BF)
        do = do.reshape(nc, cols, ctx_rows)
        dos.append(exchange_ctx(do if g == 0 else after(do, dos[0])))
    grad_out = dot(mixed, grad_attended, 1, 0).astype(BF).reshape(nc, nz, 2, rows_w, width)
    grad_out_got = core_swap(lax.dynamic_index_in_dim(grad_out, 1 - core, 2, False))
    grad_out = lax.dynamic_index_in_dim(grad_out, core, 2, False).astype(F32) + grad_out_got.astype(F32)
    mats = [t.reshape(nc, nz, 2 * rows_w, width) for t in grad_ups] + [grad_out.astype(BF)]
    grad_up = jnp.concatenate(mats, axis=2).reshape(nc, nz * (n_up + rows_w), width)
    grad_up = lax.psum_scatter(grad_up, "ctx", scatter_dimension=0).reshape(nz, n_up + rows_w, width)

    backs = []
    grad_qkv = None
    grad_bias_parts = []
    for g in range(groups):
        dqkv = attend_back(qkvs[g], dos[g], 0, lses[g], segs[g], ctx_rows)
        if g == 1:
            dqkv, backs[0], down_got = lax.optimization_barrier((dqkv, backs[0], down_got))
        grad_bias_parts.append(jnp.sum(dqkv.astype(F32), axis=1))
        back = dot(dqkv, w_qkv, 0, 1).astype(BF).reshape(nc, ctx_rows, width)
        if g + 1 < groups:
            grad_down = after(grad_down, dqkv).reshape(nz, ff_w, width)
            down_got = z_send(grad_down)
            qkvs[g + 1] = after(qkvs[g + 1], back)
        if g + 1 < groups:
            backs.append(exchange_ctx(back))
        else:
            backs.append(send_ctx([pick(back, me ^ r) for r in range(nc)]))
        now = dot(inputs_all[g], dqkv, 0, 1)
        grad_qkv = now if grad_qkv is None else grad_qkv + now
    grad_bias = sum(grad_bias_parts).reshape(3, cols)
    spread = lambda v: lax.dynamic_update_slice_in_dim(jnp.zeros((width,), F32), v, me * cols, 0)
    small = [
        spread(grad_bias[0]),
        spread(grad_bias[2]),
        grad_out_bias,
        grad_gain_one,
        grad_bias_one,
        grad_down_bias,
        grad_gain_two,
        grad_bias_two,
    ]
    small = [t.reshape(nc * nf, rows_w) for t in small]
    grad_up_bias = grad_up_bias.reshape(nc * nz, ff_w)
    pair = [jnp.where(core == j, grad_up_bias, 0.0) for j in range(2)]
    small.append(jnp.stack(pair, axis=1).reshape(nc * nf, ff_w))
    small = jnp.concatenate(small, axis=1)
    grad_qkv = grad_qkv.astype(BF).reshape(nc, nz, 2, rows_w, 3 * cols)
    grad_qkv_got = core_swap(lax.dynamic_index_in_dim(grad_qkv, 1 - core, 2, False))
    grad_qkv = lax.dynamic_index_in_dim(grad_qkv, core, 2, False).astype(F32) + grad_qkv_got.astype(F32)
    grad_qkv = jnp.moveaxis(grad_qkv.astype(BF), 1, 0)
    small = jnp.sum(lax.all_to_all(after(small, grad_qkv), BOTH, 0, 0), axis=0)
    up_got = z_send(after(grad_up, grad_qkv))
    grad_qkv = z_sum(grad_qkv, z_send(grad_qkv))
    backs_last = after(backs[-1], grad_qkv)
    grad_qkv = exchange_ctx(grad_qkv).reshape(nc, rows_w, 3, cols)
    grad_qkv = jnp.moveaxis(grad_qkv, 0, 2).reshape(rows_w, 3, width)
    input_grads = [total_of([t[r] for r in range(nc)]) for t in backs[:-1] + [backs_last]]
    grad_down = z_sum(grad_down, down_got)
    grad_up = z_sum(grad_up, up_got)
    grad_out = grad_up[n_up:]
    grad_up = [grad_up[j * 2 * rows_w : (j + 1) * 2 * rows_w] for j in range(parts)]
    grad_up = jnp.concatenate(grad_up, axis=1).reshape(2, rows_w, half)
    grad_up_got = core_swap(lax.dynamic_index_in_dim(grad_up, 1 - core, 0, False))
    pair = [
        t.reshape(rows_w, half // ff_w, ff_w)
        for t in (lax.dynamic_index_in_dim(grad_up, core, 0, False), grad_up_got)
    ]
    grad_up = in_order(pair[0], pair[1], core, 2).reshape(rows_w, ff)
    grad_tokens = grad_h1.reshape(groups, ctx_rows, width) + jnp.stack(input_grads)
    grad_tokens = grad_tokens.reshape(micro, per_device, ctx_rows, width)

    small_out = [small[j * rows_w : (j + 1) * rows_w] for j in range(8)]
    g_bq, g_bv, g_bo, g_g1, g_b1, g_bd, g_g2, g_b2 = small_out
    g_bu = small[8 * rows_w :]

    return (
        output,
        grad_tokens,
        grad_qkv[:, 0],
        g_bq,
        grad_qkv[:, 1],
        grad_qkv[:, 2],
        g_bv,
        grad_out,
        g_bo,
        g_g1,
        g_b1,
        grad_up,
        g_bu,
        grad_down,
        g_bd,
        g_g2,
        g_b2,
    )


def solution(mesh):
    stream = P(None, "fsdp", "ctx", None)
    mat = P(BOTH, None)
    vec = P(BOTH)
    return jax.shard_map(
        body,
        mesh=mesh,
        in_specs=(
            stream,
            P(None, "fsdp", None),
            mat,
            vec,
            mat,
            mat,
            vec,
            mat,
            vec,
            vec,
            vec,
            mat,
            vec,
            mat,
            vec,
            vec,
            vec,
            stream,
        ),
        out_specs=(
            stream,
            stream,
            mat,
            vec,
            mat,
            mat,
            vec,
            mat,
            vec,
            vec,
            vec,
            mat,
            vec,
            mat,
            vec,
            vec,
            vec,
        ),
        check_vma=False,
    )
```

```python
import functools

import jax
import jax.numpy as jnp
from jax import lax
from jax.experimental import pallas as pl
from jax.experimental.pallas import tpu as pltpu
from jax.sharding import PartitionSpec as P

H = 16
HD = 64
EPSILON = 1e-12
SCORE_SCALE = 0.125
MASKED = -1e30
BF = jnp.bfloat16
F32 = jnp.float32
BOTH = ("ctx", "fsdp")
VMEM_LIMIT = 48 << 20


def dot(a, b, ca, cb):
    return lax.dot_general(a, b, (((ca,), (cb,)), ((), ())), preferred_element_type=F32)


def swap(x, axis, r):
    n = lax.axis_size(axis)
    return lax.ppermute(x, axis, [(i, i ^ r) for i in range(n)])


def core_swap(x):
    return swap(x, "fsdp", 1)


def after(x, *first):
    return lax.optimization_barrier((x, first))[0]


def bits_of(n):
    return [1 << b for b in range(n.bit_length() - 1)]


def in_order(mine, got, bit, dim):
    return jnp.where(bit == 0, jnp.stack([mine, got], axis=dim), jnp.stack([got, mine], axis=dim))


def core_groups():
    n = lax.axis_size("fsdp") * lax.axis_size("ctx")
    return [list(range(k, n, 2)) for k in range(2)]


def z_groups():
    n = lax.axis_size("fsdp")
    return [list(range(k, n, 2)) for k in range(2)]


def place(pieces, me):
    n = len(pieces)
    out = jnp.zeros((n,) + pieces[0].shape, pieces[0].dtype)
    for r in range(n):
        out = lax.dynamic_update_index_in_dim(out, pieces[r], me ^ r, 0)
    return out


def pick(x, i):
    return lax.dynamic_index_in_dim(x, i, 0, False)


def gather_z(x):
    n = lax.axis_size("fsdp") // 2
    return [x] + [swap(x, "fsdp", 2 * r) for r in range(1, n)]


def gather_ctx(x, order):
    pieces = {0: x}
    for b in order:
        for r in list(pieces):
            pieces[r ^ b] = swap(pieces[r], "ctx", b)
    return [pieces[r] for r in range(len(pieces))]


def exchange_ctx(x):
    return lax.all_to_all(x, "ctx", 0, 0)


def send_ctx(chunks):
    return [chunks[0]] + [swap(c, "ctx", r) for r, c in enumerate(chunks) if r]


def total_of(pieces):
    out = pieces[0].astype(F32)
    for p in pieces[1:]:
        out = out + p.astype(F32)
    return out


def add_up(x):
    return jnp.sum(x.astype(F32), axis=0).astype(BF)


def z_send(x):
    n = lax.axis_size("fsdp") // 2
    z = lax.axis_index("fsdp") // 2
    return [swap(lax.dynamic_index_in_dim(x, z ^ r, 0, False), "fsdp", 2 * r) for r in range(1, n)]


def z_sum(x, got):
    total = lax.dynamic_index_in_dim(x, lax.axis_index("fsdp") // 2, 0, False).astype(F32)
    for g in got:
        total = total + g.astype(F32)
    return total


def exchange_ctx(x):
    return lax.all_to_all(x, "ctx", 0, 0)


def attend_kernel(q_ref, k_ref, v_ref, srow_ref, scol_ref, o_ref, lse_ref):
    q = q_ref[...] * jnp.asarray(SCORE_SCALE, BF)
    s = dot(k_ref[...], q, 0, 0)
    s = jnp.where(scol_ref[...] == srow_ref[...], s, MASKED)
    top = jnp.max(s, axis=0, keepdims=True)
    p = jnp.exp(s - top)
    total = jnp.sum(p, axis=0, keepdims=True)
    o = dot(v_ref[...], p.astype(BF), 1, 0)
    o_ref[...] = (o / total).astype(BF)[None]
    lse_ref[...] = (top + jnp.log(total))[None]


def attend(qkv, seg, block):
    rows, length = qkv.shape
    heads = rows // (3 * HD)
    nq = length // block
    whole = lambda part: pl.BlockSpec((HD, length), lambda h, i: (part * heads + h, 0))
    return pl.pallas_call(
        attend_kernel,
        grid=(heads, nq),
        in_specs=[
            pl.BlockSpec((HD, block), lambda h, i: (h, i)),
            whole(1),
            whole(2),
            pl.BlockSpec((1, block), lambda h, i: (0, i)),
            pl.BlockSpec((length, 1), lambda h, i: (0, 0)),
        ],
        out_specs=[
            pl.BlockSpec((1, HD, block), lambda h, i: (i, h, 0)),
            pl.BlockSpec((1, 1, block), lambda h, i: (h, 0, i)),
        ],
        out_shape=[
            jax.ShapeDtypeStruct((nq, heads * HD, block), BF),
            jax.ShapeDtypeStruct((heads, 1, length), F32),
        ],
        compiler_params=pltpu.CompilerParams(vmem_limit_bytes=VMEM_LIMIT),
        cost_estimate=pl.CostEstimate(
            flops=1 << 20,
            transcendentals=1 << 10,
            bytes_accessed=1 << 20,
        ),
        name="attend",
    )(qkv, qkv, qkv, seg[None, :], seg[:, None])


def attend_back_kernel(
    heads, nq, block, q_ref, k_ref, v_ref, do_ref, lse_ref, srow_ref, scol_ref, out_ref, dk_ref, dv_ref, kt_ref, vt_ref
):
    h = pl.program_id(0)
    i = pl.program_id(1)

    @pl.when(i == 0)
    def _():
        kt_ref[...] = k_ref[...].T
        vt_ref[...] = v_ref[...].T
        dk_ref[...] = jnp.zeros_like(dk_ref)
        dv_ref[...] = jnp.zeros_like(dv_ref)

    q = q_ref[...] * jnp.asarray(SCORE_SCALE, BF)
    do = do_ref[0]
    p = jnp.exp(dot(kt_ref[...], q, 1, 0) - lse_ref[0])
    p = jnp.where(scol_ref[...] == srow_ref[...], p, 0.0)
    dp = dot(vt_ref[...], do, 1, 0)
    central = jnp.sum(p * dp, axis=0, keepdims=True)
    ds = (p * (dp - central)).astype(BF)
    dq = dot(k_ref[...], ds, 1, 0) * SCORE_SCALE
    out_ref[pl.ds(pl.multiple_of(h * HD, HD), HD), pl.ds(pl.multiple_of(i * block, block), block)] = dq.astype(BF)
    dk_ref[...] += dot(ds, q.T, 1, 0)
    dv_ref[...] += dot(p.astype(BF), do.T, 1, 0)

    @pl.when(i == nq - 1)
    def _():
        out_ref[pl.ds(pl.multiple_of((heads + h) * HD, HD), HD), :] = dk_ref[...].T.astype(BF)
        out_ref[pl.ds(pl.multiple_of((2 * heads + h) * HD, HD), HD), :] = dv_ref[...].T.astype(BF)


def attend_back(qkv, do, group, lse, seg, block):
    rows, length = qkv.shape
    heads = rows // (3 * HD)
    nq = length // block
    whole = lambda part: pl.BlockSpec((HD, length), lambda h, i: (part * heads + h, 0))
    return pl.pallas_call(
        functools.partial(attend_back_kernel, heads, nq, block),
        grid=(heads, nq),
        in_specs=[
            pl.BlockSpec((HD, block), lambda h, i: (h, i)),
            whole(1),
            whole(2),
            pl.BlockSpec((1, HD, block), lambda h, i: (i, h, group)),
            pl.BlockSpec((1, 1, block), lambda h, i: (h, 0, i)),
            pl.BlockSpec((1, block), lambda h, i: (0, i)),
            pl.BlockSpec((length, 1), lambda h, i: (0, 0)),
        ],
        out_specs=pl.BlockSpec((rows, length), lambda h, i: (0, 0)),
        out_shape=jax.ShapeDtypeStruct((rows, length), BF),
        scratch_shapes=[pltpu.VMEM((length, HD), F32)] * 2 + [pltpu.VMEM((length, HD), BF)] * 2,
        compiler_params=pltpu.CompilerParams(vmem_limit_bytes=VMEM_LIMIT),
        cost_estimate=pl.CostEstimate(
            flops=1 << 20,
            transcendentals=1 << 10,
            bytes_accessed=1 << 20,
        ),
        name="attend_back",
    )(qkv, qkv, qkv, do, lse, seg[None, :], seg[:, None])


def norm_forward(values_in, gain_vec, bias_vec):
    center = values_in - jnp.mean(values_in, axis=-1, keepdims=True)
    inverse = lax.rsqrt(jnp.mean(center * center, axis=-1, keepdims=True) + EPSILON)
    normed = center * inverse
    return (normed * gain_vec + bias_vec, normed, inverse)


def norm_backward(upstream, normed, inverse, gain_vec):
    scaled = upstream * gain_vec
    inner_sum = (
        scaled
        - jnp.mean(scaled, axis=-1, keepdims=True)
        - normed * jnp.mean(scaled * normed, axis=-1, keepdims=True)
    )
    return (inverse * inner_sum, jnp.sum(upstream * normed, axis=0), jnp.sum(upstream, axis=0))


def segment_ids(lengths, positions):
    starts = jnp.cumsum(lengths) - lengths
    return jnp.sum((positions[:, None] >= starts[None, :]).astype(jnp.int32), axis=1) - 1


def body(
    tokens,
    doc_lengths,
    w_query,
    b_query,
    w_key,
    w_value,
    b_value,
    w_out,
    b_out,
    ln1_gain,
    ln1_bias,
    w_up,
    b_up,
    w_down,
    b_down,
    ln2_gain,
    ln2_bias,
    cotangent,
):
    micro, per_device, ctx_rows, width = tokens.shape
    nc = lax.axis_size("ctx")
    nf = lax.axis_size("fsdp")
    nz = nf // 2
    me = lax.axis_index("ctx")
    fi = lax.axis_index("fsdp")
    core = fi % 2
    rows_w = w_query.shape[0]
    ff_w = w_down.shape[0]
    ff = w_up.shape[1]
    half = ff // 2
    cols = width // nc
    length = ctx_rows * nc
    flat_rows = micro * per_device * ctx_rows
    groups = micro * per_device
    order_a = bits_of(nc)
    order_b = order_a[::-1]
    me_c, me_z = me, fi // 2

    w_qkv = jnp.stack([w_query, w_key, w_value], axis=1).reshape(rows_w, 3, nc, cols)
    w_qkv = jnp.moveaxis(w_qkv, 2, 0).reshape(nc, rows_w, 3 * cols)
    vectors = (b_query, b_value, b_out, ln1_gain, ln1_bias, b_down, ln2_gain, ln2_bias, b_up)
    packed = jnp.concatenate(vectors)
    packed = jnp.pad(packed, (0, 8 * 3 * cols - packed.shape[0])).reshape(1, 8, 3 * cols)
    sent = jnp.concatenate([w_qkv, jnp.broadcast_to(packed, (nc, 8, 3 * cols))], axis=1)
    sent_c = send_ctx([pick(sent, me ^ r) for r in range(nc)])
    sent_z = gather_z(place(sent_c, me_c))
    mine = tokens.reshape(groups, ctx_rows, width)
    inputs_all = []
    for g in range(groups):
        rows_now = after(mine[g], sent_c) if g == 0 else after(mine[g], inputs_all[g - 1])
        inputs_all.append(exchange_ctx(jnp.broadcast_to(rows_now[None], (nc, ctx_rows, width))))
    inputs_all = [t.reshape(length, width) for t in inputs_all]
    sent = place(sent_z, me_z)
    sent = in_order(sent, core_swap(sent), core, 2)
    sent = jnp.moveaxis(sent, 0, 1)
    w_qkv = sent[:, :, :, :rows_w].reshape(width, 3 * cols)
    packed = sent[:, :, :, rows_w:].reshape(nc * nf, 8 * 3 * cols)
    full = [packed[:, j * rows_w : (j + 1) * rows_w].reshape(width) for j in range(8)]
    query_bias, value_bias, out_bias, gain_one, bias_one, down_bias, gain_two, bias_two = full
    up_bias = packed[:, 8 * rows_w : 8 * rows_w + ff_w].reshape(nc * nz, 2, ff_w)
    up_bias = lax.dynamic_index_in_dim(up_bias, core, 1, False).reshape(half)

    split = w_up.reshape(rows_w, half // ff_w, 2, ff_w)
    keep = lax.dynamic_index_in_dim(split, core, 2, False).reshape(rows_w, half)
    give = lax.dynamic_index_in_dim(split, 1 - core, 2, False).reshape(rows_w, half)
    up_mine = in_order(keep, core_swap(give), core, 0).reshape(2 * rows_w, half)
    parts = half // width
    own = jnp.concatenate([up_mine[:, j * width : (j + 1) * width] for j in range(parts)] + [w_down])
    own = lax.all_gather(own, BOTH, axis=0, axis_index_groups=core_groups())

    key_pos = jnp.arange(length, dtype=jnp.int32)
    lengths = doc_lengths.reshape(groups, -1)
    zero_bias = jnp.zeros((cols,), BF)
    qkv_bias = jnp.concatenate(
        [
            lax.dynamic_slice_in_dim(query_bias, me * cols, cols),
            zero_bias,
            lax.dynamic_slice_in_dim(value_bias, me * cols, cols),
        ]
    ).astype(F32)[:, None]
    segs, qkvs, lses, mixed = [], [], [], []
    outs = []
    for g in range(groups):
        segs.append(segment_ids(lengths[g], key_pos))
        rows_now = inputs_all[g] if g == 0 else after(inputs_all[g], outs[0])
        qkvs.append((dot(w_qkv, rows_now, 0, 1) + qkv_bias).astype(BF))
        o, lse = attend(qkvs[g], segs[g], ctx_rows)
        outs.append(o)
        lses.append(lse)
        mixed.append(exchange_ctx(o if g == 0 else after(o, mixed[-1])))
    out_c = send_ctx([place(gather_z(after(w_out, outs[0])), me_z)] * nc)
    out_mat = place(after(out_c, outs[-1]), me_c)
    out_mat = in_order(out_mat, core_swap(out_mat), core, 2).reshape(width, width)
    own = after(own, mixed[-1])
    mixed = jnp.concatenate([t.reshape(width, ctx_rows) for t in mixed], axis=1)
    n_up = 2 * rows_w * parts
    up_mat = jnp.concatenate(
        [own[:, j * 2 * rows_w : (j + 1) * 2 * rows_w].reshape(width, width) for j in range(parts)], axis=1
    )
    down_mat = own[:, n_up : n_up + ff_w].reshape(half, width)
    inputs = mine.reshape(flat_rows, width).astype(F32)
    attended = dot(mixed, out_mat, 0, 0) + out_bias
    first, normed_one, inverse_one = norm_forward(inputs + attended, gain_one, bias_one)
    first_low = first.astype(BF)
    both_first = jnp.concatenate([first_low, core_swap(first_low)])
    hidden = dot(both_first, up_mat, 1, 0) + up_bias
    cdf = 0.5 * (1.0 + lax.erf(hidden * 0.7071067811865476))
    slope = (cdf + hidden * jnp.exp(-0.5 * hidden * hidden) * 0.3989422804014327).astype(BF)
    activated = (hidden * cdf).astype(BF)
    away = core_swap(dot(activated[flat_rows:], down_mat, 1, 0).astype(BF))
    branch = dot(activated[:flat_rows], down_mat, 1, 0) + away.astype(F32) + down_bias
    result, normed_two, inverse_two = norm_forward(first + branch, gain_two, bias_two)
    output = result.astype(BF).reshape(micro, per_device, ctx_rows, width)

    upstream = cotangent.reshape(flat_rows, width).astype(F32)
    grad_h2, grad_gain_two, grad_bias_two = norm_backward(upstream, normed_two, inverse_two, gain_two)
    grad_branch = grad_h2.astype(BF)
    grad_down_bias = jnp.sum(grad_branch.astype(F32), axis=0)
    both_branch = jnp.concatenate([grad_branch, core_swap(grad_branch)])
    grad_down = dot(activated, both_branch, 0, 0).astype(BF)
    both_branch = lax.optimization_barrier((both_branch, grad_down))[0]
    grad_down = lax.psum_scatter(grad_down, "ctx", scatter_dimension=0, tiled=True)
    grad_hidden = (dot(both_branch, down_mat, 1, 1) * slope.astype(F32)).astype(BF)
    grad_up_bias = dot(jnp.ones((8, grad_hidden.shape[0]), BF), grad_hidden, 1, 0)[0]
    away = core_swap(dot(grad_hidden[flat_rows:], up_mat, 1, 1).astype(BF))
    grad_first = dot(grad_hidden[:flat_rows], up_mat, 1, 1) + away.astype(F32) + grad_h2
    grad_h1, grad_gain_one, grad_bias_one = norm_backward(grad_first, normed_one, inverse_one, gain_one)
    grad_attended = grad_h1.astype(BF)
    grad_out_bias = jnp.sum(grad_attended.astype(F32), axis=0)
    dos = []
    for g in range(groups):
        do = dot(out_mat, grad_attended[g * ctx_rows : (g + 1) * ctx_rows], 1, 1).astype(BF)
        dos.append(do.reshape(nc, cols, ctx_rows))
    for g in range(groups):
        dos[g] = exchange_ctx(dos[g] if g == 0 else after(dos[g], dos[0]))
    later = after((both_first, grad_hidden, mixed, grad_attended), dos[0])
    grad_out = dot(later[2], later[3], 1, 0).astype(BF).reshape(nc, nz, 2, rows_w, width)
    grad_ups = [
        dot(later[0], later[1][:, j * width : (j + 1) * width], 0, 0).astype(BF) for j in range(parts)
    ]
    grad_out_got = core_swap(lax.dynamic_index_in_dim(grad_out, 1 - core, 2, False))
    grad_out = lax.dynamic_index_in_dim(grad_out, core, 2, False).astype(F32) + grad_out_got.astype(F32)
    mats = [t.reshape(nc, nz, 2 * rows_w, width) for t in grad_ups] + [grad_out.astype(BF)]
    grad_up = jnp.concatenate(mats, axis=2).reshape(nc, nz * (n_up + rows_w), width)
    grad_up = lax.psum_scatter(grad_up, "ctx", scatter_dimension=0).reshape(nz, n_up + rows_w, width)

    backs = []
    grad_qkv = None
    grad_bias_parts = []
    for g in range(groups):
        dqkv = attend_back(qkvs[g], dos[g], 0, lses[g], segs[g], ctx_rows)
        if g == 1:
            dqkv, backs[0], down_got = lax.optimization_barrier((dqkv, backs[0], down_got))
        grad_bias_parts.append(jnp.sum(dqkv.astype(F32), axis=1))
        back = dot(dqkv, w_qkv, 0, 1).astype(BF).reshape(nc, ctx_rows, width)
        if g + 1 < groups:
            grad_down = after(grad_down, dqkv).reshape(nz, ff_w, width)
            down_got = z_send(grad_down)
            qkvs[g + 1] = after(qkvs[g + 1], back)
        if g + 1 < groups:
            backs.append(exchange_ctx(back))
        else:
            backs.append(send_ctx([pick(back, me ^ r) for r in range(nc)]))
        now = dot(inputs_all[g], dqkv, 0, 1)
        grad_qkv = now if grad_qkv is None else grad_qkv + now
    grad_bias = sum(grad_bias_parts).reshape(3, cols)
    spread = lambda v: lax.dynamic_update_slice_in_dim(jnp.zeros((width,), F32), v, me * cols, 0)
    small = [
        spread(grad_bias[0]),
        spread(grad_bias[2]),
        grad_out_bias,
        grad_gain_one,
        grad_bias_one,
        grad_down_bias,
        grad_gain_two,
        grad_bias_two,
    ]
    small = [t.reshape(nc * nf, rows_w) for t in small]
    grad_up_bias = grad_up_bias.reshape(nc * nz, ff_w)
    pair = [jnp.where(core == j, grad_up_bias, 0.0) for j in range(2)]
    small.append(jnp.stack(pair, axis=1).reshape(nc * nf, ff_w))
    small = jnp.concatenate(small, axis=1)
    small = jnp.pad(small, ((0, 0), (0, 8 * 3 * cols - small.shape[1]))).astype(BF)
    small = small.reshape(nc, nz, 2, 8, 3 * cols)
    grad_qkv = grad_qkv.astype(BF).reshape(nc, nz, 2, rows_w, 3 * cols)
    grad_qkv = jnp.concatenate([grad_qkv, small], axis=3)
    grad_qkv_got = core_swap(lax.dynamic_index_in_dim(grad_qkv, 1 - core, 2, False))
    grad_qkv = lax.dynamic_index_in_dim(grad_qkv, core, 2, False).astype(F32) + grad_qkv_got.astype(F32)
    grad_qkv = jnp.moveaxis(grad_qkv.astype(BF), 1, 0)
    grad_qkv = z_sum(grad_qkv, z_send(grad_qkv)).astype(BF)
    backs[-1] = after(backs[-1], grad_qkv)
    got = send_ctx([pick(grad_qkv, me ^ r) for r in range(nc)])
    small = total_of([t[rows_w:] for t in got]).reshape(8 * 3 * cols)
    grad_qkv = place([t[:rows_w] for t in got], me_c).reshape(nc, rows_w, 3, cols)
    grad_qkv = jnp.moveaxis(grad_qkv, 0, 2).reshape(rows_w, 3, width).astype(F32)
    grad_up = lax.psum_scatter(grad_up, "fsdp", scatter_dimension=0, axis_index_groups=z_groups()).astype(F32)
    input_grads = [total_of([t[r] for r in range(nc)]) for t in backs]
    grad_down = z_sum(grad_down, down_got)
    grad_out = grad_up[n_up:]
    grad_up = [grad_up[j * 2 * rows_w : (j + 1) * 2 * rows_w] for j in range(parts)]
    grad_up = jnp.concatenate(grad_up, axis=1).reshape(2, rows_w, half)
    grad_up_got = core_swap(lax.dynamic_index_in_dim(grad_up, 1 - core, 0, False))
    pair = [
        t.reshape(rows_w, half // ff_w, ff_w)
        for t in (lax.dynamic_index_in_dim(grad_up, core, 0, False), grad_up_got)
    ]
    grad_up = in_order(pair[0], pair[1], core, 2).reshape(rows_w, ff)
    grad_tokens = grad_h1.reshape(groups, ctx_rows, width) + jnp.stack(input_grads)
    grad_tokens = grad_tokens.reshape(micro, per_device, ctx_rows, width)

    small_out = [small[j * rows_w : (j + 1) * rows_w] for j in range(8)]
    g_bq, g_bv, g_bo, g_g1, g_b1, g_bd, g_g2, g_b2 = small_out
    g_bu = small[8 * rows_w : 8 * rows_w + ff_w]

    return (
        output,
        grad_tokens,
        grad_qkv[:, 0],
        g_bq,
        grad_qkv[:, 1],
        grad_qkv[:, 2],
        g_bv,
        grad_out,
        g_bo,
        g_g1,
        g_b1,
        grad_up,
        g_bu,
        grad_down,
        g_bd,
        g_g2,
        g_b2,
    )


def solution(mesh):
    stream = P(None, "fsdp", "ctx", None)
    mat = P(BOTH, None)
    vec = P(BOTH)
    return jax.shard_map(
        body,
        mesh=mesh,
        in_specs=(
            stream,
            P(None, "fsdp", None),
            mat,
            vec,
            mat,
            mat,
            vec,
            mat,
            vec,
            vec,
            vec,
            mat,
            vec,
            mat,
            vec,
            vec,
            vec,
            stream,
        ),
        out_specs=(
            stream,
            stream,
            mat,
            vec,
            mat,
            mat,
            vec,
            mat,
            vec,
            vec,
            vec,
            mat,
            vec,
            mat,
            vec,
            vec,
            vec,
        ),
        check_vma=False,
    )
```

```python
import functools

import jax
import jax.numpy as jnp
from jax import lax
from jax.experimental import pallas as pl
from jax.experimental.pallas import tpu as pltpu
from jax.sharding import PartitionSpec as P

H = 16
HD = 64
EPSILON = 1e-12
SCORE_SCALE = 0.125
MASKED = -1e30
BF = jnp.bfloat16
F32 = jnp.float32
BOTH = ("ctx", "fsdp")
VMEM_LIMIT = 16 << 20


def dot(a, b, ca, cb):
    return lax.dot_general(a, b, (((ca,), (cb,)), ((), ())), preferred_element_type=F32)


def swap(x, axis, r):
    n = lax.axis_size(axis)
    return lax.ppermute(x, axis, [(i, i ^ r) for i in range(n)])


def core_swap(x):
    return swap(x, "fsdp", 1)


def after(x, *first):
    return lax.optimization_barrier((x, first))[0]


def bits_of(n):
    return [1 << b for b in range(n.bit_length() - 1)]


def in_order(mine, got, bit, dim):
    return jnp.where(bit == 0, jnp.stack([mine, got], axis=dim), jnp.stack([got, mine], axis=dim))


def core_groups():
    n = lax.axis_size("fsdp") * lax.axis_size("ctx")
    return [list(range(k, n, 2)) for k in range(2)]


def z_groups():
    n = lax.axis_size("fsdp")
    return [list(range(k, n, 2)) for k in range(2)]


def place(pieces, me):
    n = len(pieces)
    out = jnp.zeros((n,) + pieces[0].shape, pieces[0].dtype)
    for r in range(n):
        out = lax.dynamic_update_index_in_dim(out, pieces[r], me ^ r, 0)
    return out


def pick(x, i):
    return lax.dynamic_index_in_dim(x, i, 0, False)


def gather_z(x):
    n = lax.axis_size("fsdp") // 2
    return [x] + [swap(x, "fsdp", 2 * r) for r in range(1, n)]


def gather_ctx(x, order):
    pieces = {0: x}
    for b in order:
        for r in list(pieces):
            pieces[r ^ b] = swap(pieces[r], "ctx", b)
    return [pieces[r] for r in range(len(pieces))]


def exchange_ctx(x):
    return lax.all_to_all(x, "ctx", 0, 0)


def send_ctx(chunks):
    return [chunks[0]] + [swap(c, "ctx", r) for r, c in enumerate(chunks) if r]


def total_of(pieces):
    out = pieces[0].astype(F32)
    for p in pieces[1:]:
        out = out + p.astype(F32)
    return out


def add_up(x):
    return jnp.sum(x.astype(F32), axis=0).astype(BF)


def z_send(x):
    n = lax.axis_size("fsdp") // 2
    z = lax.axis_index("fsdp") // 2
    return [swap(lax.dynamic_index_in_dim(x, z ^ r, 0, False), "fsdp", 2 * r) for r in range(1, n)]


def z_sum(x, got):
    total = lax.dynamic_index_in_dim(x, lax.axis_index("fsdp") // 2, 0, False).astype(F32)
    for g in got:
        total = total + g.astype(F32)
    return total


def exchange_ctx(x):
    return lax.all_to_all(x, "ctx", 0, 0)


def attend_kernel(q_ref, k_ref, v_ref, srow_ref, scol_ref, o_ref, lse_ref):
    q = q_ref[...] * jnp.asarray(SCORE_SCALE, BF)
    s = dot(k_ref[...], q, 0, 0)
    s = jnp.where(scol_ref[...] == srow_ref[...], s, MASKED)
    top = jnp.max(s, axis=0, keepdims=True)
    p = jnp.exp(s - top)
    total = jnp.sum(p, axis=0, keepdims=True)
    o = dot(v_ref[...], p.astype(BF), 1, 0)
    o_ref[...] = (o / total).astype(BF)[None]
    lse_ref[...] = (top + jnp.log(total))[None]


def attend(qkv, seg, block):
    rows, length = qkv.shape
    heads = rows // (3 * HD)
    nq = length // block
    whole = lambda part: pl.BlockSpec((HD, length), lambda h, i: (part * heads + h, 0))
    return pl.pallas_call(
        attend_kernel,
        grid=(heads, nq),
        in_specs=[
            pl.BlockSpec((HD, block), lambda h, i: (h, i)),
            whole(1),
            whole(2),
            pl.BlockSpec((1, block), lambda h, i: (0, i)),
            pl.BlockSpec((length, 1), lambda h, i: (0, 0)),
        ],
        out_specs=[
            pl.BlockSpec((1, HD, block), lambda h, i: (i, h, 0)),
            pl.BlockSpec((1, 1, block), lambda h, i: (h, 0, i)),
        ],
        out_shape=[
            jax.ShapeDtypeStruct((nq, heads * HD, block), BF),
            jax.ShapeDtypeStruct((heads, 1, length), F32),
        ],
        compiler_params=pltpu.CompilerParams(vmem_limit_bytes=VMEM_LIMIT),
        cost_estimate=pl.CostEstimate(
            flops=1 << 20,
            transcendentals=1 << 10,
            bytes_accessed=1 << 20,
        ),
        name="attend",
    )(qkv, qkv, qkv, seg[None, :], seg[:, None])


def attend_back_kernel(
    heads, nq, block, q_ref, k_ref, v_ref, do_ref, lse_ref, srow_ref, scol_ref, out_ref, dk_ref, dv_ref, kt_ref, vt_ref
):
    h = pl.program_id(0)
    i = pl.program_id(1)

    @pl.when(i == 0)
    def _():
        kt_ref[...] = k_ref[...].T
        vt_ref[...] = v_ref[...].T
        dk_ref[...] = jnp.zeros_like(dk_ref)
        dv_ref[...] = jnp.zeros_like(dv_ref)

    q = q_ref[...] * jnp.asarray(SCORE_SCALE, BF)
    do = do_ref[0]
    p = jnp.exp(dot(kt_ref[...], q, 1, 0) - lse_ref[0])
    p = jnp.where(scol_ref[...] == srow_ref[...], p, 0.0)
    dp = dot(vt_ref[...], do, 1, 0)
    central = jnp.sum(p * dp, axis=0, keepdims=True)
    ds = (p * (dp - central)).astype(BF)
    dq = dot(k_ref[...], ds, 1, 0) * SCORE_SCALE
    out_ref[pl.ds(pl.multiple_of(h * HD, HD), HD), pl.ds(pl.multiple_of(i * block, block), block)] = dq.astype(BF)
    dk_ref[...] += dot(ds, q.T, 1, 0)
    dv_ref[...] += dot(p.astype(BF), do.T, 1, 0)

    @pl.when(i == nq - 1)
    def _():
        out_ref[pl.ds(pl.multiple_of((heads + h) * HD, HD), HD), :] = dk_ref[...].T.astype(BF)
        out_ref[pl.ds(pl.multiple_of((2 * heads + h) * HD, HD), HD), :] = dv_ref[...].T.astype(BF)


def attend_back(qkv, do, group, lse, seg, block):
    rows, length = qkv.shape
    heads = rows // (3 * HD)
    nq = length // block
    whole = lambda part: pl.BlockSpec((HD, length), lambda h, i: (part * heads + h, 0))
    return pl.pallas_call(
        functools.partial(attend_back_kernel, heads, nq, block),
        grid=(heads, nq),
        in_specs=[
            pl.BlockSpec((HD, block), lambda h, i: (h, i)),
            whole(1),
            whole(2),
            pl.BlockSpec((1, HD, block), lambda h, i: (i, h, group)),
            pl.BlockSpec((1, 1, block), lambda h, i: (h, 0, i)),
            pl.BlockSpec((1, block), lambda h, i: (0, i)),
            pl.BlockSpec((length, 1), lambda h, i: (0, 0)),
        ],
        out_specs=pl.BlockSpec((rows, length), lambda h, i: (0, 0)),
        out_shape=jax.ShapeDtypeStruct((rows, length), BF),
        scratch_shapes=[pltpu.VMEM((length, HD), F32)] * 2 + [pltpu.VMEM((length, HD), BF)] * 2,
        compiler_params=pltpu.CompilerParams(vmem_limit_bytes=VMEM_LIMIT),
        cost_estimate=pl.CostEstimate(
            flops=1 << 20,
            transcendentals=1 << 10,
            bytes_accessed=1 << 20,
        ),
        name="attend_back",
    )(qkv, qkv, qkv, do, lse, seg[None, :], seg[:, None])


def norm_forward(values_in, gain_vec, bias_vec):
    center = values_in - jnp.mean(values_in, axis=-1, keepdims=True)
    inverse = lax.rsqrt(jnp.mean(center * center, axis=-1, keepdims=True) + EPSILON)
    normed = center * inverse
    return (normed * gain_vec + bias_vec, normed, inverse)


def norm_backward(upstream, normed, inverse, gain_vec):
    scaled = upstream * gain_vec
    inner_sum = (
        scaled
        - jnp.mean(scaled, axis=-1, keepdims=True)
        - normed * jnp.mean(scaled * normed, axis=-1, keepdims=True)
    )
    return (inverse * inner_sum, jnp.sum(upstream * normed, axis=0), jnp.sum(upstream, axis=0))


def segment_ids(lengths, positions):
    starts = jnp.cumsum(lengths) - lengths
    return jnp.sum((positions[:, None] >= starts[None, :]).astype(jnp.int32), axis=1) - 1


def body(
    tokens,
    doc_lengths,
    w_query,
    b_query,
    w_key,
    w_value,
    b_value,
    w_out,
    b_out,
    ln1_gain,
    ln1_bias,
    w_up,
    b_up,
    w_down,
    b_down,
    ln2_gain,
    ln2_bias,
    cotangent,
):
    micro, per_device, ctx_rows, width = tokens.shape
    nc = lax.axis_size("ctx")
    nf = lax.axis_size("fsdp")
    nz = nf // 2
    me = lax.axis_index("ctx")
    fi = lax.axis_index("fsdp")
    core = fi % 2
    rows_w = w_query.shape[0]
    ff_w = w_down.shape[0]
    ff = w_up.shape[1]
    half = ff // 2
    cols = width // nc
    length = ctx_rows * nc
    flat_rows = micro * per_device * ctx_rows
    groups = micro * per_device
    order_a = bits_of(nc)
    order_b = order_a[::-1]
    me_c, me_z = me, fi // 2

    w_qkv = jnp.stack([w_query, w_key, w_value], axis=1).reshape(rows_w, 3, nc, cols)
    w_qkv = jnp.moveaxis(w_qkv, 2, 0).reshape(nc, rows_w, 3 * cols)
    vectors = (b_query, b_value, b_out, ln1_gain, ln1_bias, b_down, ln2_gain, ln2_bias, b_up)
    packed = jnp.concatenate(vectors)
    packed = jnp.pad(packed, (0, 8 * 3 * cols - packed.shape[0])).reshape(1, 8, 3 * cols)
    sent = jnp.concatenate([w_qkv, jnp.broadcast_to(packed, (nc, 8, 3 * cols))], axis=1)
    sent_c = send_ctx([pick(sent, me ^ r) for r in range(nc)])
    sent_z = gather_z(place(sent_c, me_c))
    mine = tokens.reshape(groups, ctx_rows, width)
    inputs_all = []
    for g in range(groups):
        rows_now = after(mine[g], sent_c) if g == 0 else after(mine[g], inputs_all[g - 1])
        inputs_all.append(exchange_ctx(jnp.broadcast_to(rows_now[None], (nc, ctx_rows, width))))
    inputs_all = [t.reshape(length, width) for t in inputs_all]
    sent = place(sent_z, me_z)
    sent = in_order(sent, core_swap(sent), core, 2)
    sent = jnp.moveaxis(sent, 0, 1)
    w_qkv = sent[:, :, :, :rows_w].reshape(width, 3 * cols)
    packed = sent[:, :, :, rows_w:].reshape(nc * nf, 8 * 3 * cols)
    full = [packed[:, j * rows_w : (j + 1) * rows_w].reshape(width) for j in range(8)]
    query_bias, value_bias, out_bias, gain_one, bias_one, down_bias, gain_two, bias_two = full
    up_bias = packed[:, 8 * rows_w : 8 * rows_w + ff_w].reshape(nc * nz, 2, ff_w)
    up_bias = lax.dynamic_index_in_dim(up_bias, core, 1, False).reshape(half)

    split = w_up.reshape(rows_w, half // ff_w, 2, ff_w)
    keep = lax.dynamic_index_in_dim(split, core, 2, False).reshape(rows_w, half)
    give = lax.dynamic_index_in_dim(split, 1 - core, 2, False).reshape(rows_w, half)
    up_mine = in_order(keep, core_swap(give), core, 0).reshape(2 * rows_w, half)
    parts = half // width
    own = jnp.concatenate([up_mine[:, j * width : (j + 1) * width] for j in range(parts)] + [w_down])
    own = lax.all_gather(own, BOTH, axis=0, axis_index_groups=core_groups())

    key_pos = jnp.arange(length, dtype=jnp.int32)
    lengths = doc_lengths.reshape(groups, -1)
    zero_bias = jnp.zeros((cols,), BF)
    qkv_bias = jnp.concatenate(
        [
            lax.dynamic_slice_in_dim(query_bias, me * cols, cols),
            zero_bias,
            lax.dynamic_slice_in_dim(value_bias, me * cols, cols),
        ]
    ).astype(F32)[:, None]
    segs, qkvs, lses, mixed = [], [], [], []
    outs = []
    for g in range(groups):
        segs.append(segment_ids(lengths[g], key_pos))
        rows_now = inputs_all[g] if g == 0 else after(inputs_all[g], outs[0])
        qkvs.append((dot(w_qkv, rows_now, 0, 1) + qkv_bias).astype(BF))
        o, lse = attend(qkvs[g], segs[g], ctx_rows)
        outs.append(o)
        lses.append(lse)
        mixed.append(exchange_ctx(o if g == 0 else after(o, mixed[-1])))
    out_c = send_ctx([place(gather_z(after(w_out, outs[0])), me_z)] * nc)
    out_mat = place(after(out_c, outs[-1]), me_c)
    out_mat = in_order(out_mat, core_swap(out_mat), core, 2).reshape(width, width)
    own = after(own, mixed[-1])
    mixed = jnp.concatenate([t.reshape(width, ctx_rows) for t in mixed], axis=1)
    n_up = 2 * rows_w * parts
    up_mat = jnp.concatenate(
        [own[:, j * 2 * rows_w : (j + 1) * 2 * rows_w].reshape(width, width) for j in range(parts)], axis=1
    )
    down_mat = own[:, n_up : n_up + ff_w].reshape(half, width)
    inputs = mine.reshape(flat_rows, width).astype(F32)
    attended = dot(mixed, out_mat, 0, 0) + out_bias
    first, normed_one, inverse_one = norm_forward(inputs + attended, gain_one, bias_one)
    first_low = first.astype(BF)
    both_first = jnp.concatenate([first_low, core_swap(first_low)])
    hidden = dot(both_first, up_mat, 1, 0) + up_bias
    cdf = 0.5 * (1.0 + lax.erf(hidden * 0.7071067811865476))
    slope = (cdf + hidden * jnp.exp(-0.5 * hidden * hidden) * 0.3989422804014327).astype(BF)
    activated = (hidden * cdf).astype(BF)
    away = core_swap(dot(activated[flat_rows:], down_mat, 1, 0).astype(BF))
    branch = dot(activated[:flat_rows], down_mat, 1, 0) + away.astype(F32) + down_bias
    result, normed_two, inverse_two = norm_forward(first + branch, gain_two, bias_two)
    output = result.astype(BF).reshape(micro, per_device, ctx_rows, width)

    upstream = cotangent.reshape(flat_rows, width).astype(F32)
    grad_h2, grad_gain_two, grad_bias_two = norm_backward(upstream, normed_two, inverse_two, gain_two)
    grad_branch = grad_h2.astype(BF)
    grad_down_bias = jnp.sum(grad_branch.astype(F32), axis=0)
    other_branch = core_swap(grad_branch)
    hidden_own = (dot(grad_branch, down_mat, 1, 1) * slope[:flat_rows].astype(F32)).astype(BF)
    grad_down = dot(activated, jnp.concatenate([grad_branch, other_branch]), 0, 0).astype(BF)
    other_branch = lax.optimization_barrier((other_branch, grad_down))[0]
    grad_down = lax.psum_scatter(grad_down, "ctx", scatter_dimension=0, tiled=True)
    hidden_other = (dot(other_branch, down_mat, 1, 1) * slope[flat_rows:].astype(F32)).astype(BF)
    grad_hidden = jnp.concatenate([hidden_own, hidden_other])
    grad_up_bias = dot(jnp.ones((8, grad_hidden.shape[0]), BF), grad_hidden, 1, 0)[0]
    away = core_swap(dot(hidden_other, up_mat, 1, 1).astype(BF))
    grad_first = dot(hidden_own, up_mat, 1, 1) + away.astype(F32) + grad_h2
    grad_h1, grad_gain_one, grad_bias_one = norm_backward(grad_first, normed_one, inverse_one, gain_one)
    grad_attended = grad_h1.astype(BF)
    grad_out_bias = jnp.sum(grad_attended.astype(F32), axis=0)
    do_all = exchange_ctx(dot(out_mat, grad_attended, 1, 1).astype(BF).reshape(nc, cols, flat_rows))
    later = after((both_first, grad_hidden, mixed, grad_attended), do_all)
    grad_out = dot(later[2], later[3], 1, 0).astype(BF).reshape(nc, nz, 2, rows_w, width)
    grad_ups = [
        dot(later[0], later[1][:, j * width : (j + 1) * width], 0, 0).astype(BF) for j in range(parts)
    ]
    grad_out_got = core_swap(lax.dynamic_index_in_dim(grad_out, 1 - core, 2, False))
    grad_out = lax.dynamic_index_in_dim(grad_out, core, 2, False).astype(F32) + grad_out_got.astype(F32)
    mats = [t.reshape(nc, nz, 2 * rows_w, width) for t in grad_ups] + [grad_out.astype(BF)]
    grad_up = jnp.concatenate(mats, axis=2).reshape(nc, nz * (n_up + rows_w), width)
    grad_up = lax.psum_scatter(grad_up, "ctx", scatter_dimension=0).reshape(nz, n_up + rows_w, width)

    backs = []
    grad_qkv = None
    grad_bias_parts = []
    for g in range(groups):
        dqkv = attend_back(qkvs[g], do_all, g, lses[g], segs[g], ctx_rows)
        if g == 1:
            dqkv, backs[0], down_got = lax.optimization_barrier((dqkv, backs[0], down_got))
        grad_bias_parts.append(jnp.sum(dqkv.astype(F32), axis=1))
        back = dot(dqkv, w_qkv, 0, 1).astype(BF).reshape(nc, ctx_rows, width)
        if g + 1 < groups:
            grad_down = after(grad_down, dqkv).reshape(nz, ff_w, width)
            down_got = z_send(grad_down)
            qkvs[g + 1] = after(qkvs[g + 1], back)
        if g + 1 < groups:
            backs.append(exchange_ctx(back))
        else:
            backs.append(send_ctx([pick(back, me ^ r) for r in range(nc)]))
        now = dot(inputs_all[g], dqkv, 0, 1)
        grad_qkv = now if grad_qkv is None else grad_qkv + now
    grad_bias = sum(grad_bias_parts).reshape(3, cols)
    spread = lambda v: lax.dynamic_update_slice_in_dim(jnp.zeros((width,), F32), v, me * cols, 0)
    small = [
        spread(grad_bias[0]),
        spread(grad_bias[2]),
        grad_out_bias,
        grad_gain_one,
        grad_bias_one,
        grad_down_bias,
        grad_gain_two,
        grad_bias_two,
    ]
    small = [t.reshape(nc * nf, rows_w) for t in small]
    grad_up_bias = grad_up_bias.reshape(nc * nz, ff_w)
    pair = [jnp.where(core == j, grad_up_bias, 0.0) for j in range(2)]
    small.append(jnp.stack(pair, axis=1).reshape(nc * nf, ff_w))
    small = jnp.concatenate(small, axis=1)
    small = jnp.pad(small, ((0, 0), (0, 8 * 3 * cols - small.shape[1]))).astype(BF)
    small = small.reshape(nc, nz, 2, 8, 3 * cols)
    grad_qkv = grad_qkv.astype(BF).reshape(nc, nz, 2, rows_w, 3 * cols)
    grad_qkv = jnp.concatenate([grad_qkv, small], axis=3)
    grad_qkv_got = core_swap(lax.dynamic_index_in_dim(grad_qkv, 1 - core, 2, False))
    grad_qkv = lax.dynamic_index_in_dim(grad_qkv, core, 2, False).astype(F32) + grad_qkv_got.astype(F32)
    grad_qkv = jnp.moveaxis(grad_qkv.astype(BF), 1, 0)
    grad_qkv = z_sum(grad_qkv, z_send(grad_qkv)).astype(BF)
    backs[-1] = after(backs[-1], grad_qkv)
    got = send_ctx([pick(grad_qkv, me ^ r) for r in range(nc)])
    small = total_of([t[rows_w:] for t in got]).reshape(8 * 3 * cols)
    grad_qkv = place([t[:rows_w] for t in got], me_c).reshape(nc, rows_w, 3, cols)
    grad_qkv = jnp.moveaxis(grad_qkv, 0, 2).reshape(rows_w, 3, width).astype(F32)
    grad_up = lax.psum_scatter(grad_up, "fsdp", scatter_dimension=0, axis_index_groups=z_groups())
    input_grads = [total_of([t[r] for r in range(nc)]) for t in backs]
    grad_down = z_sum(grad_down, down_got)
    grad_out = grad_up[n_up:].astype(F32)
    grad_up = [grad_up[j * 2 * rows_w : (j + 1) * 2 * rows_w] for j in range(parts)]
    grad_up = jnp.concatenate(grad_up, axis=1).reshape(2, rows_w, half)
    grad_up_got = core_swap(lax.dynamic_index_in_dim(grad_up, 1 - core, 0, False))
    pair = [
        t.reshape(rows_w, half // ff_w, ff_w)
        for t in (lax.dynamic_index_in_dim(grad_up, core, 0, False), grad_up_got)
    ]
    grad_up = in_order(pair[0], pair[1], core, 2).reshape(rows_w, ff).astype(F32)
    grad_tokens = grad_h1.reshape(groups, ctx_rows, width) + jnp.stack(input_grads)
    grad_tokens = grad_tokens.reshape(micro, per_device, ctx_rows, width)

    small_out = [small[j * rows_w : (j + 1) * rows_w] for j in range(8)]
    g_bq, g_bv, g_bo, g_g1, g_b1, g_bd, g_g2, g_b2 = small_out
    g_bu = small[8 * rows_w : 8 * rows_w + ff_w]

    return (
        output,
        grad_tokens,
        grad_qkv[:, 0],
        g_bq,
        grad_qkv[:, 1],
        grad_qkv[:, 2],
        g_bv,
        grad_out,
        g_bo,
        g_g1,
        g_b1,
        grad_up,
        g_bu,
        grad_down,
        g_bd,
        g_g2,
        g_b2,
    )


def solution(mesh):
    stream = P(None, "fsdp", "ctx", None)
    mat = P(BOTH, None)
    vec = P(BOTH)
    return jax.shard_map(
        body,
        mesh=mesh,
        in_specs=(
            stream,
            P(None, "fsdp", None),
            mat,
            vec,
            mat,
            mat,
            vec,
            mat,
            vec,
            vec,
            vec,
            mat,
            vec,
            mat,
            vec,
            vec,
            vec,
            stream,
        ),
        out_specs=(
            stream,
            stream,
            mat,
            vec,
            mat,
            mat,
            vec,
            mat,
            vec,
            vec,
            vec,
            mat,
            vec,
            mat,
            vec,
            vec,
            vec,
        ),
        check_vma=False,
    )
```

```python
import functools

import jax
import jax.numpy as jnp
from jax import lax
from jax.experimental import pallas as pl
from jax.experimental.pallas import tpu as pltpu
from jax.sharding import PartitionSpec as P

H = 16
HD = 64
EPSILON = 1e-12
SCORE_SCALE = 0.125
MASKED = -1e30
BF = jnp.bfloat16
F32 = jnp.float32
BOTH = ("ctx", "fsdp")
VMEM_LIMIT = 16 << 20


def dot(a, b, ca, cb):
    return lax.dot_general(a, b, (((ca,), (cb,)), ((), ())), preferred_element_type=F32)


def swap(x, axis, r):
    n = lax.axis_size(axis)
    return lax.ppermute(x, axis, [(i, i ^ r) for i in range(n)])


def core_swap(x):
    return swap(x, "fsdp", 1)


def after(x, *first):
    return lax.optimization_barrier((x, first))[0]


def bits_of(n):
    return [1 << b for b in range(n.bit_length() - 1)]


def in_order(mine, got, bit, dim):
    return jnp.where(bit == 0, jnp.stack([mine, got], axis=dim), jnp.stack([got, mine], axis=dim))


def core_groups():
    n = lax.axis_size("fsdp") * lax.axis_size("ctx")
    return [list(range(k, n, 2)) for k in range(2)]


def z_groups():
    n = lax.axis_size("fsdp")
    return [list(range(k, n, 2)) for k in range(2)]


def place(pieces, me):
    n = len(pieces)
    out = jnp.zeros((n,) + pieces[0].shape, pieces[0].dtype)
    for r in range(n):
        out = lax.dynamic_update_index_in_dim(out, pieces[r], me ^ r, 0)
    return out


def pick(x, i):
    return lax.dynamic_index_in_dim(x, i, 0, False)


def gather_z(x):
    n = lax.axis_size("fsdp") // 2
    return [x] + [swap(x, "fsdp", 2 * r) for r in range(1, n)]


def gather_ctx(x, order):
    pieces = {0: x}
    for b in order:
        for r in list(pieces):
            pieces[r ^ b] = swap(pieces[r], "ctx", b)
    return [pieces[r] for r in range(len(pieces))]


def exchange_ctx(x):
    return lax.all_to_all(x, "ctx", 0, 0)


def send_ctx(chunks):
    return [chunks[0]] + [swap(c, "ctx", r) for r, c in enumerate(chunks) if r]


def total_of(pieces):
    out = pieces[0].astype(F32)
    for p in pieces[1:]:
        out = out + p.astype(F32)
    return out


def add_up(x):
    return jnp.sum(x.astype(F32), axis=0).astype(BF)


def z_send(x):
    n = lax.axis_size("fsdp") // 2
    z = lax.axis_index("fsdp") // 2
    return [swap(lax.dynamic_index_in_dim(x, z ^ r, 0, False), "fsdp", 2 * r) for r in range(1, n)]


def z_sum(x, got):
    total = lax.dynamic_index_in_dim(x, lax.axis_index("fsdp") // 2, 0, False).astype(F32)
    for g in got:
        total = total + g.astype(F32)
    return total


def exchange_ctx(x):
    return lax.all_to_all(x, "ctx", 0, 0)


def attend_kernel(q_ref, k_ref, v_ref, srow_ref, scol_ref, o_ref, lse_ref):
    q = q_ref[...] * jnp.asarray(SCORE_SCALE, BF)
    s = dot(k_ref[...], q, 0, 0)
    s = jnp.where(scol_ref[...] == srow_ref[...], s, MASKED)
    top = jnp.max(s, axis=0, keepdims=True)
    p = jnp.exp(s - top)
    total = jnp.sum(p, axis=0, keepdims=True)
    o = dot(v_ref[...], p.astype(BF), 1, 0)
    o_ref[...] = (o / total).astype(BF)[None]
    lse_ref[...] = (top + jnp.log(total))[None]


def attend(qkv, seg, block):
    rows, length = qkv.shape
    heads = rows // (3 * HD)
    nq = length // block
    whole = lambda part: pl.BlockSpec((HD, length), lambda h, i: (part * heads + h, 0))
    return pl.pallas_call(
        attend_kernel,
        grid=(heads, nq),
        in_specs=[
            pl.BlockSpec((HD, block), lambda h, i: (h, i)),
            whole(1),
            whole(2),
            pl.BlockSpec((1, block), lambda h, i: (0, i)),
            pl.BlockSpec((length, 1), lambda h, i: (0, 0)),
        ],
        out_specs=[
            pl.BlockSpec((1, HD, block), lambda h, i: (i, h, 0)),
            pl.BlockSpec((1, 1, block), lambda h, i: (h, 0, i)),
        ],
        out_shape=[
            jax.ShapeDtypeStruct((nq, heads * HD, block), BF),
            jax.ShapeDtypeStruct((heads, 1, length), F32),
        ],
        compiler_params=pltpu.CompilerParams(vmem_limit_bytes=VMEM_LIMIT),
        cost_estimate=pl.CostEstimate(
            flops=12000 << 20,
            transcendentals=1 << 10,
            bytes_accessed=1 << 20,
        ),
        name="attend",
    )(qkv, qkv, qkv, seg[None, :], seg[:, None])


def attend_back_kernel(
    heads, nq, block, q_ref, k_ref, v_ref, do_ref, lse_ref, srow_ref, scol_ref, out_ref, dk_ref, dv_ref, kt_ref, vt_ref
):
    h = pl.program_id(0)
    i = pl.program_id(1)

    @pl.when(i == 0)
    def _():
        kt_ref[...] = k_ref[...].T
        vt_ref[...] = v_ref[...].T
        dk_ref[...] = jnp.zeros_like(dk_ref)
        dv_ref[...] = jnp.zeros_like(dv_ref)

    q = q_ref[...] * jnp.asarray(SCORE_SCALE, BF)
    do = do_ref[0]
    p = jnp.exp(dot(kt_ref[...], q, 1, 0) - lse_ref[0])
    p = jnp.where(scol_ref[...] == srow_ref[...], p, 0.0)
    dp = dot(vt_ref[...], do, 1, 0)
    central = jnp.sum(p * dp, axis=0, keepdims=True)
    ds = (p * (dp - central)).astype(BF)
    dq = dot(k_ref[...], ds, 1, 0) * SCORE_SCALE
    out_ref[pl.ds(pl.multiple_of(h * HD, HD), HD), pl.ds(pl.multiple_of(i * block, block), block)] = dq.astype(BF)
    dk_ref[...] += dot(ds, q.T, 1, 0)
    dv_ref[...] += dot(p.astype(BF), do.T, 1, 0)

    @pl.when(i == nq - 1)
    def _():
        out_ref[pl.ds(pl.multiple_of((heads + h) * HD, HD), HD), :] = dk_ref[...].T.astype(BF)
        out_ref[pl.ds(pl.multiple_of((2 * heads + h) * HD, HD), HD), :] = dv_ref[...].T.astype(BF)


def attend_back(qkv, do, group, lse, seg, block):
    rows, length = qkv.shape
    heads = rows // (3 * HD)
    nq = length // block
    whole = lambda part: pl.BlockSpec((HD, length), lambda h, i: (part * heads + h, 0))
    return pl.pallas_call(
        functools.partial(attend_back_kernel, heads, nq, block),
        grid=(heads, nq),
        in_specs=[
            pl.BlockSpec((HD, block), lambda h, i: (h, i)),
            whole(1),
            whole(2),
            pl.BlockSpec((1, HD, block), lambda h, i: (i, h, group)),
            pl.BlockSpec((1, 1, block), lambda h, i: (h, 0, i)),
            pl.BlockSpec((1, block), lambda h, i: (0, i)),
            pl.BlockSpec((length, 1), lambda h, i: (0, 0)),
        ],
        out_specs=pl.BlockSpec((rows, length), lambda h, i: (0, 0)),
        out_shape=jax.ShapeDtypeStruct((rows, length), BF),
        scratch_shapes=[pltpu.VMEM((length, HD), F32)] * 2 + [pltpu.VMEM((length, HD), BF)] * 2,
        compiler_params=pltpu.CompilerParams(vmem_limit_bytes=VMEM_LIMIT),
        cost_estimate=pl.CostEstimate(
            flops=1 << 20,
            transcendentals=1 << 10,
            bytes_accessed=1 << 20,
        ),
        name="attend_back",
    )(qkv, qkv, qkv, do, lse, seg[None, :], seg[:, None])


def norm_forward(values_in, gain_vec, bias_vec):
    center = values_in - jnp.mean(values_in, axis=-1, keepdims=True)
    inverse = lax.rsqrt(jnp.mean(center * center, axis=-1, keepdims=True) + EPSILON)
    normed = center * inverse
    return (normed * gain_vec + bias_vec, normed, inverse)


def norm_backward(upstream, normed, inverse, gain_vec):
    scaled = upstream * gain_vec
    inner_sum = (
        scaled
        - jnp.mean(scaled, axis=-1, keepdims=True)
        - normed * jnp.mean(scaled * normed, axis=-1, keepdims=True)
    )
    return (inverse * inner_sum, jnp.sum(upstream * normed, axis=0), jnp.sum(upstream, axis=0))


def segment_ids(lengths, positions):
    starts = jnp.cumsum(lengths) - lengths
    return jnp.sum((positions[:, None] >= starts[None, :]).astype(jnp.int32), axis=1) - 1


def body(
    tokens,
    doc_lengths,
    w_query,
    b_query,
    w_key,
    w_value,
    b_value,
    w_out,
    b_out,
    ln1_gain,
    ln1_bias,
    w_up,
    b_up,
    w_down,
    b_down,
    ln2_gain,
    ln2_bias,
    cotangent,
):
    micro, per_device, ctx_rows, width = tokens.shape
    nc = lax.axis_size("ctx")
    nf = lax.axis_size("fsdp")
    nz = nf // 2
    me = lax.axis_index("ctx")
    fi = lax.axis_index("fsdp")
    core = fi % 2
    rows_w = w_query.shape[0]
    ff_w = w_down.shape[0]
    ff = w_up.shape[1]
    half = ff // 2
    cols = width // nc
    length = ctx_rows * nc
    flat_rows = micro * per_device * ctx_rows
    groups = micro * per_device
    order_a = bits_of(nc)
    order_b = order_a[::-1]
    me_c, me_z = me, fi // 2

    w_qkv = jnp.stack([w_query, w_key, w_value], axis=1).reshape(rows_w, 3, nc, cols)
    w_qkv = jnp.moveaxis(w_qkv, 2, 0).reshape(nc, rows_w, 3 * cols)
    vectors = (b_query, b_value, b_out, ln1_gain, ln1_bias, b_down, ln2_gain, ln2_bias, b_up)
    packed = jnp.concatenate(vectors)
    packed = jnp.pad(packed, (0, 8 * 3 * cols - packed.shape[0])).reshape(1, 8, 3 * cols)
    sent = jnp.concatenate([w_qkv, jnp.broadcast_to(packed, (nc, 8, 3 * cols))], axis=1)
    sent_c = send_ctx([pick(sent, me ^ r) for r in range(nc)])
    sent_z = gather_z(place(sent_c, me_c))
    mine = tokens.reshape(groups, ctx_rows, width)
    inputs_all = []
    for g in range(groups):
        rows_now = after(mine[g], sent_c) if g == 0 else after(mine[g], inputs_all[g - 1])
        inputs_all.append(exchange_ctx(jnp.broadcast_to(rows_now[None], (nc, ctx_rows, width))))
    inputs_all = [t.reshape(length, width) for t in inputs_all]
    sent = place(sent_z, me_z)
    sent = in_order(sent, core_swap(sent), core, 2)
    sent = jnp.moveaxis(sent, 0, 1)
    w_qkv = sent[:, :, :, :rows_w].reshape(width, 3 * cols)
    packed = sent[:, :, :, rows_w:].reshape(nc * nf, 8 * 3 * cols)
    full = [packed[:, j * rows_w : (j + 1) * rows_w].reshape(width) for j in range(8)]
    query_bias, value_bias, out_bias, gain_one, bias_one, down_bias, gain_two, bias_two = full
    up_bias = packed[:, 8 * rows_w : 8 * rows_w + ff_w].reshape(nc * nz, 2, ff_w)
    up_bias = lax.dynamic_index_in_dim(up_bias, core, 1, False).reshape(half)

    split = w_up.reshape(rows_w, half // ff_w, 2, ff_w)
    keep = lax.dynamic_index_in_dim(split, core, 2, False).reshape(rows_w, half)
    give = lax.dynamic_index_in_dim(split, 1 - core, 2, False).reshape(rows_w, half)
    up_mine = in_order(keep, core_swap(give), core, 0).reshape(2 * rows_w, half)
    parts = half // width
    own = jnp.concatenate([up_mine[:, j * width : (j + 1) * width] for j in range(parts)] + [w_down])
    own = lax.all_gather(own, BOTH, axis=0, axis_index_groups=core_groups())

    key_pos = jnp.arange(length, dtype=jnp.int32)
    lengths = doc_lengths.reshape(groups, -1)
    zero_bias = jnp.zeros((cols,), BF)
    qkv_bias = jnp.concatenate(
        [
            lax.dynamic_slice_in_dim(query_bias, me * cols, cols),
            zero_bias,
            lax.dynamic_slice_in_dim(value_bias, me * cols, cols),
        ]
    ).astype(F32)[:, None]
    segs, qkvs, lses, mixed = [], [], [], []
    outs = []
    for g in range(groups):
        segs.append(segment_ids(lengths[g], key_pos))
        rows_now = inputs_all[g] if g == 0 else after(inputs_all[g], outs[0])
        qkvs.append((dot(w_qkv, rows_now, 0, 1) + qkv_bias).astype(BF))
        o, lse = attend(qkvs[g], segs[g], ctx_rows)
        outs.append(o)
        lses.append(lse)
        mixed.append(exchange_ctx(o if g == 0 else after(o, mixed[-1])))
    out_c = send_ctx([place(gather_z(after(w_out, outs[0])), me_z)] * nc)
    out_mat = place(after(out_c, outs[-1]), me_c)
    out_mat = in_order(out_mat, core_swap(out_mat), core, 2).reshape(width, width)
    own = after(own, mixed[-1])
    mixed = jnp.concatenate([t.reshape(width, ctx_rows) for t in mixed], axis=1)
    n_up = 2 * rows_w * parts
    up_mat = jnp.concatenate(
        [own[:, j * 2 * rows_w : (j + 1) * 2 * rows_w].reshape(width, width) for j in range(parts)], axis=1
    )
    down_mat = own[:, n_up : n_up + ff_w].reshape(half, width)
    inputs = mine.reshape(flat_rows, width).astype(F32)
    attended = dot(mixed, out_mat, 0, 0) + out_bias
    first, normed_one, inverse_one = norm_forward(inputs + attended, gain_one, bias_one)
    first_low = first.astype(BF)
    both_first = jnp.concatenate([first_low, core_swap(first_low)])
    hidden = dot(both_first, up_mat, 1, 0) + up_bias
    cdf = 0.5 * (1.0 + lax.erf(hidden * 0.7071067811865476))
    slope = (cdf + hidden * jnp.exp(-0.5 * hidden * hidden) * 0.3989422804014327).astype(BF)
    activated = (hidden * cdf).astype(BF)
    away = core_swap(dot(activated[flat_rows:], down_mat, 1, 0).astype(BF))
    branch = dot(activated[:flat_rows], down_mat, 1, 0) + away.astype(F32) + down_bias
    result, normed_two, inverse_two = norm_forward(first + branch, gain_two, bias_two)
    output = result.astype(BF).reshape(micro, per_device, ctx_rows, width)

    upstream = cotangent.reshape(flat_rows, width).astype(F32)
    grad_h2, grad_gain_two, grad_bias_two = norm_backward(upstream, normed_two, inverse_two, gain_two)
    grad_branch = grad_h2.astype(BF)
    grad_down_bias = jnp.sum(grad_branch.astype(F32), axis=0)
    other_branch = core_swap(grad_branch)
    hidden_own = (dot(grad_branch, down_mat, 1, 1) * slope[:flat_rows].astype(F32)).astype(BF)
    grad_down = dot(activated, jnp.concatenate([grad_branch, other_branch]), 0, 0).astype(BF)
    other_branch = lax.optimization_barrier((other_branch, grad_down))[0]
    grad_down = lax.psum_scatter(grad_down, "ctx", scatter_dimension=0, tiled=True)
    hidden_other = (dot(other_branch, down_mat, 1, 1) * slope[flat_rows:].astype(F32)).astype(BF)
    grad_hidden = jnp.concatenate([hidden_own, hidden_other])
    grad_up_bias = dot(jnp.ones((8, grad_hidden.shape[0]), BF), grad_hidden, 1, 0)[0]
    away = core_swap(dot(hidden_other, up_mat, 1, 1).astype(BF))
    grad_first = dot(hidden_own, up_mat, 1, 1) + away.astype(F32) + grad_h2
    grad_h1, grad_gain_one, grad_bias_one = norm_backward(grad_first, normed_one, inverse_one, gain_one)
    grad_attended = grad_h1.astype(BF)
    grad_out_bias = jnp.sum(grad_attended.astype(F32), axis=0)
    do_all = exchange_ctx(dot(out_mat, grad_attended, 1, 1).astype(BF).reshape(nc, cols, flat_rows))
    later = after((both_first, grad_hidden, mixed, grad_attended), do_all)
    grad_out = dot(later[2], later[3], 1, 0).astype(BF).reshape(nc, nz, 2, rows_w, width)
    grad_ups = [
        dot(later[0], later[1][:, j * width : (j + 1) * width], 0, 0).astype(BF) for j in range(parts)
    ]
    grad_out_got = core_swap(lax.dynamic_index_in_dim(grad_out, 1 - core, 2, False))
    grad_out = lax.dynamic_index_in_dim(grad_out, core, 2, False).astype(F32) + grad_out_got.astype(F32)
    mats = [t.reshape(nc, nz, 2 * rows_w, width) for t in grad_ups] + [grad_out.astype(BF)]
    grad_up = jnp.concatenate(mats, axis=2).reshape(nc, nz * (n_up + rows_w), width)
    grad_up = lax.psum_scatter(grad_up, "ctx", scatter_dimension=0).reshape(nz, n_up + rows_w, width)

    backs = []
    grad_qkv = None
    grad_bias_parts = []
    for g in range(groups):
        dqkv = attend_back(qkvs[g], do_all, g, lses[g], segs[g], ctx_rows)
        if g == 1:
            dqkv, backs[0], down_got = lax.optimization_barrier((dqkv, backs[0], down_got))
        grad_bias_parts.append(jnp.sum(dqkv.astype(F32), axis=1))
        back = dot(dqkv, w_qkv, 0, 1).astype(BF).reshape(nc, ctx_rows, width)
        if g + 1 < groups:
            grad_down = after(grad_down, dqkv).reshape(nz, ff_w, width)
            down_got = z_send(grad_down)
            qkvs[g + 1] = after(qkvs[g + 1], back)
        if g + 1 < groups:
            backs.append(exchange_ctx(back))
        else:
            backs.append(send_ctx([pick(back, me ^ r) for r in range(nc)]))
        now = dot(inputs_all[g], dqkv, 0, 1)
        grad_qkv = now if grad_qkv is None else grad_qkv + now
    grad_bias = sum(grad_bias_parts).reshape(3, cols)
    spread = lambda v: lax.dynamic_update_slice_in_dim(jnp.zeros((width,), F32), v, me * cols, 0)
    small = [
        spread(grad_bias[0]),
        spread(grad_bias[2]),
        grad_out_bias,
        grad_gain_one,
        grad_bias_one,
        grad_down_bias,
        grad_gain_two,
        grad_bias_two,
    ]
    small = [t.reshape(nc * nf, rows_w) for t in small]
    grad_up_bias = grad_up_bias.reshape(nc * nz, ff_w)
    pair = [jnp.where(core == j, grad_up_bias, 0.0) for j in range(2)]
    small.append(jnp.stack(pair, axis=1).reshape(nc * nf, ff_w))
    small = jnp.concatenate(small, axis=1)
    small = jnp.pad(small, ((0, 0), (0, 8 * 3 * cols - small.shape[1]))).astype(BF)
    small = small.reshape(nc, nz, 2, 8, 3 * cols)
    grad_qkv = grad_qkv.astype(BF).reshape(nc, nz, 2, rows_w, 3 * cols)
    grad_qkv = jnp.concatenate([grad_qkv, small], axis=3)
    grad_qkv_got = core_swap(lax.dynamic_index_in_dim(grad_qkv, 1 - core, 2, False))
    grad_qkv = lax.dynamic_index_in_dim(grad_qkv, core, 2, False).astype(F32) + grad_qkv_got.astype(F32)
    grad_qkv = jnp.moveaxis(grad_qkv.astype(BF), 1, 0)
    grad_qkv = z_sum(grad_qkv, z_send(grad_qkv)).astype(BF)
    backs[-1] = after(backs[-1], grad_qkv)
    got = send_ctx([pick(grad_qkv, me ^ r) for r in range(nc)])
    small = total_of([t[rows_w:] for t in got]).reshape(8 * 3 * cols)
    grad_qkv = place([t[:rows_w] for t in got], me_c).reshape(nc, rows_w, 3, cols)
    grad_qkv = jnp.moveaxis(grad_qkv, 0, 2).reshape(rows_w, 3, width).astype(F32)
    grad_up = lax.psum_scatter(grad_up, "fsdp", scatter_dimension=0, axis_index_groups=z_groups())
    input_grads = [total_of([t[r] for r in range(nc)]) for t in backs]
    grad_down = z_sum(grad_down, down_got)
    grad_out = grad_up[n_up:].astype(F32)
    grad_up = [grad_up[j * 2 * rows_w : (j + 1) * 2 * rows_w] for j in range(parts)]
    grad_up = jnp.concatenate(grad_up, axis=1).reshape(2, rows_w, half)
    grad_up_got = core_swap(lax.dynamic_index_in_dim(grad_up, 1 - core, 0, False))
    pair = [
        t.reshape(rows_w, half // ff_w, ff_w)
        for t in (lax.dynamic_index_in_dim(grad_up, core, 0, False), grad_up_got)
    ]
    grad_up = in_order(pair[0], pair[1], core, 2).reshape(rows_w, ff).astype(F32)
    grad_tokens = grad_h1.reshape(groups, ctx_rows, width) + jnp.stack(input_grads)
    grad_tokens = grad_tokens.reshape(micro, per_device, ctx_rows, width)

    small_out = [small[j * rows_w : (j + 1) * rows_w] for j in range(8)]
    g_bq, g_bv, g_bo, g_g1, g_b1, g_bd, g_g2, g_b2 = small_out
    g_bu = small[8 * rows_w : 8 * rows_w + ff_w]

    return (
        output,
        grad_tokens,
        grad_qkv[:, 0],
        g_bq,
        grad_qkv[:, 1],
        grad_qkv[:, 2],
        g_bv,
        grad_out,
        g_bo,
        g_g1,
        g_b1,
        grad_up,
        g_bu,
        grad_down,
        g_bd,
        g_g2,
        g_b2,
    )


def solution(mesh):
    stream = P(None, "fsdp", "ctx", None)
    mat = P(BOTH, None)
    vec = P(BOTH)
    return jax.shard_map(
        body,
        mesh=mesh,
        in_specs=(
            stream,
            P(None, "fsdp", None),
            mat,
            vec,
            mat,
            mat,
            vec,
            mat,
            vec,
            vec,
            vec,
            mat,
            vec,
            mat,
            vec,
            vec,
            vec,
            stream,
        ),
        out_specs=(
            stream,
            stream,
            mat,
            vec,
            mat,
            mat,
            vec,
            mat,
            vec,
            vec,
            vec,
            mat,
            vec,
            mat,
            vec,
            vec,
            vec,
        ),
        check_vma=False,
    )
```

```python
import functools

import jax
import jax.numpy as jnp
from jax import lax
from jax.experimental import pallas as pl
from jax.experimental.pallas import tpu as pltpu
from jax.sharding import PartitionSpec as P

H = 16
HD = 64
EPSILON = 1e-12
SCORE_SCALE = 0.125
MASKED = -1e30
BF = jnp.bfloat16
F32 = jnp.float32
BOTH = ("ctx", "fsdp")
VMEM_LIMIT = 16 << 20


def dot(a, b, ca, cb):
    return lax.dot_general(a, b, (((ca,), (cb,)), ((), ())), preferred_element_type=F32)


def swap(x, axis, r):
    n = lax.axis_size(axis)
    return lax.ppermute(x, axis, [(i, i ^ r) for i in range(n)])


def core_swap(x):
    return swap(x, "fsdp", 1)


def after(x, *first):
    return lax.optimization_barrier((x, first))[0]


def bits_of(n):
    return [1 << b for b in range(n.bit_length() - 1)]


def in_order(mine, got, bit, dim):
    return jnp.where(bit == 0, jnp.stack([mine, got], axis=dim), jnp.stack([got, mine], axis=dim))


def core_groups():
    n = lax.axis_size("fsdp") * lax.axis_size("ctx")
    return [list(range(k, n, 2)) for k in range(2)]


def z_groups():
    n = lax.axis_size("fsdp")
    return [list(range(k, n, 2)) for k in range(2)]


def place(pieces, me):
    n = len(pieces)
    out = jnp.zeros((n,) + pieces[0].shape, pieces[0].dtype)
    for r in range(n):
        out = lax.dynamic_update_index_in_dim(out, pieces[r], me ^ r, 0)
    return out


def pick(x, i):
    return lax.dynamic_index_in_dim(x, i, 0, False)


def gather_z(x):
    n = lax.axis_size("fsdp") // 2
    return [x] + [swap(x, "fsdp", 2 * r) for r in range(1, n)]


def gather_ctx(x, order):
    pieces = {0: x}
    for b in order:
        for r in list(pieces):
            pieces[r ^ b] = swap(pieces[r], "ctx", b)
    return [pieces[r] for r in range(len(pieces))]


def exchange_ctx(x):
    return lax.all_to_all(x, "ctx", 0, 0)


def send_ctx(chunks):
    return [chunks[0]] + [swap(c, "ctx", r) for r, c in enumerate(chunks) if r]


def total_of(pieces):
    out = pieces[0].astype(F32)
    for p in pieces[1:]:
        out = out + p.astype(F32)
    return out


def add_up(x):
    return jnp.sum(x.astype(F32), axis=0).astype(BF)


def z_send(x):
    n = lax.axis_size("fsdp") // 2
    z = lax.axis_index("fsdp") // 2
    return [swap(lax.dynamic_index_in_dim(x, z ^ r, 0, False), "fsdp", 2 * r) for r in range(1, n)]


def z_sum(x, got):
    total = lax.dynamic_index_in_dim(x, lax.axis_index("fsdp") // 2, 0, False).astype(F32)
    for g in got:
        total = total + g.astype(F32)
    return total


def exchange_ctx(x):
    return lax.all_to_all(x, "ctx", 0, 0)


def attend_kernel(q_ref, k_ref, v_ref, srow_ref, scol_ref, o_ref, lse_ref):
    q = q_ref[...] * jnp.asarray(SCORE_SCALE, BF)
    s = dot(k_ref[...], q, 0, 0)
    s = jnp.where(scol_ref[...] == srow_ref[...], s, MASKED)
    top = jnp.max(s, axis=0, keepdims=True)
    p = jnp.exp(s - top)
    total = jnp.sum(p, axis=0, keepdims=True)
    o = dot(v_ref[...], p.astype(BF), 1, 0)
    o_ref[...] = (o / total).astype(BF)[None]
    lse_ref[...] = (top + jnp.log(total))[None]


def attend(qkv, seg, block):
    rows, length = qkv.shape
    heads = rows // (3 * HD)
    nq = length // block
    whole = lambda part: pl.BlockSpec((HD, length), lambda h, i: (part * heads + h, 0))
    return pl.pallas_call(
        attend_kernel,
        grid=(heads, nq),
        in_specs=[
            pl.BlockSpec((HD, block), lambda h, i: (h, i)),
            whole(1),
            whole(2),
            pl.BlockSpec((1, block), lambda h, i: (0, i)),
            pl.BlockSpec((length, 1), lambda h, i: (0, 0)),
        ],
        out_specs=[
            pl.BlockSpec((1, HD, block), lambda h, i: (i, h, 0)),
            pl.BlockSpec((1, 1, block), lambda h, i: (h, 0, i)),
        ],
        out_shape=[
            jax.ShapeDtypeStruct((nq, heads * HD, block), BF),
            jax.ShapeDtypeStruct((heads, 1, length), F32),
        ],
        compiler_params=pltpu.CompilerParams(vmem_limit_bytes=VMEM_LIMIT),
        cost_estimate=pl.CostEstimate(
            flops=12000 << 20,
            transcendentals=1 << 10,
            bytes_accessed=1 << 20,
        ),
        name="attend",
    )(qkv, qkv, qkv, seg[None, :], seg[:, None])


def attend_back_kernel(
    heads, nq, block, q_ref, k_ref, v_ref, do_ref, lse_ref, srow_ref, scol_ref, out_ref, dk_ref, dv_ref, kt_ref, vt_ref
):
    h = pl.program_id(0)
    i = pl.program_id(1)

    @pl.when(i == 0)
    def _():
        kt_ref[...] = k_ref[...].T
        vt_ref[...] = v_ref[...].T
        dk_ref[...] = jnp.zeros_like(dk_ref)
        dv_ref[...] = jnp.zeros_like(dv_ref)

    q = q_ref[...] * jnp.asarray(SCORE_SCALE, BF)
    do = do_ref[0]
    p = jnp.exp(dot(kt_ref[...], q, 1, 0) - lse_ref[0])
    p = jnp.where(scol_ref[...] == srow_ref[...], p, 0.0)
    dp = dot(vt_ref[...], do, 1, 0)
    central = jnp.sum(p * dp, axis=0, keepdims=True)
    ds = (p * (dp - central)).astype(BF)
    dq = dot(k_ref[...], ds, 1, 0) * SCORE_SCALE
    out_ref[pl.ds(pl.multiple_of(h * HD, HD), HD), pl.ds(pl.multiple_of(i * block, block), block)] = dq.astype(BF)
    dk_ref[...] += dot(ds, q.T, 1, 0)
    dv_ref[...] += dot(p.astype(BF), do.T, 1, 0)

    @pl.when(i == nq - 1)
    def _():
        out_ref[pl.ds(pl.multiple_of((heads + h) * HD, HD), HD), :] = dk_ref[...].T.astype(BF)
        out_ref[pl.ds(pl.multiple_of((2 * heads + h) * HD, HD), HD), :] = dv_ref[...].T.astype(BF)


def attend_back(qkv, do, group, lse, seg, block):
    rows, length = qkv.shape
    heads = rows // (3 * HD)
    nq = length // block
    whole = lambda part: pl.BlockSpec((HD, length), lambda h, i: (part * heads + h, 0))
    return pl.pallas_call(
        functools.partial(attend_back_kernel, heads, nq, block),
        grid=(heads, nq),
        in_specs=[
            pl.BlockSpec((HD, block), lambda h, i: (h, i)),
            whole(1),
            whole(2),
            pl.BlockSpec((1, HD, block), lambda h, i: (i, h, group)),
            pl.BlockSpec((1, 1, block), lambda h, i: (h, 0, i)),
            pl.BlockSpec((1, block), lambda h, i: (0, i)),
            pl.BlockSpec((length, 1), lambda h, i: (0, 0)),
        ],
        out_specs=pl.BlockSpec((rows, length), lambda h, i: (0, 0)),
        out_shape=jax.ShapeDtypeStruct((rows, length), BF),
        scratch_shapes=[pltpu.VMEM((length, HD), F32)] * 2 + [pltpu.VMEM((length, HD), BF)] * 2,
        compiler_params=pltpu.CompilerParams(vmem_limit_bytes=VMEM_LIMIT),
        cost_estimate=pl.CostEstimate(
            flops=1 << 20,
            transcendentals=1 << 10,
            bytes_accessed=1 << 20,
        ),
        name="attend_back",
    )(qkv, qkv, qkv, do, lse, seg[None, :], seg[:, None])


def norm_forward(values_in, gain_vec, bias_vec):
    center = values_in - jnp.mean(values_in, axis=-1, keepdims=True)
    inverse = lax.rsqrt(jnp.mean(center * center, axis=-1, keepdims=True) + EPSILON)
    normed = center * inverse
    return (normed * gain_vec + bias_vec, normed, inverse)


def norm_backward(upstream, normed, inverse, gain_vec):
    scaled = upstream * gain_vec
    inner_sum = (
        scaled
        - jnp.mean(scaled, axis=-1, keepdims=True)
        - normed * jnp.mean(scaled * normed, axis=-1, keepdims=True)
    )
    return (inverse * inner_sum, jnp.sum(upstream * normed, axis=0), jnp.sum(upstream, axis=0))


def segment_ids(lengths, positions):
    starts = jnp.cumsum(lengths) - lengths
    return jnp.sum((positions[:, None] >= starts[None, :]).astype(jnp.int32), axis=1) - 1


def body(
    tokens,
    doc_lengths,
    w_query,
    b_query,
    w_key,
    w_value,
    b_value,
    w_out,
    b_out,
    ln1_gain,
    ln1_bias,
    w_up,
    b_up,
    w_down,
    b_down,
    ln2_gain,
    ln2_bias,
    cotangent,
):
    micro, per_device, ctx_rows, width = tokens.shape
    nc = lax.axis_size("ctx")
    nf = lax.axis_size("fsdp")
    nz = nf // 2
    me = lax.axis_index("ctx")
    fi = lax.axis_index("fsdp")
    core = fi % 2
    rows_w = w_query.shape[0]
    ff_w = w_down.shape[0]
    ff = w_up.shape[1]
    half = ff // 2
    cols = width // nc
    length = ctx_rows * nc
    flat_rows = micro * per_device * ctx_rows
    groups = micro * per_device
    order_a = bits_of(nc)
    order_b = order_a[::-1]
    me_c, me_z = me, fi // 2

    w_qkv = jnp.stack([w_query, w_key, w_value], axis=1).reshape(rows_w, 3, nc, cols)
    w_qkv = jnp.moveaxis(w_qkv, 2, 0).reshape(nc, rows_w, 3 * cols)
    vectors = (b_query, b_value, b_out, ln1_gain, ln1_bias, b_down, ln2_gain, ln2_bias, b_up)
    packed = jnp.concatenate(vectors)
    packed = jnp.pad(packed, (0, 8 * 3 * cols - packed.shape[0])).reshape(1, 8, 3 * cols)
    sent = jnp.concatenate([w_qkv, jnp.broadcast_to(packed, (nc, 8, 3 * cols))], axis=1)
    sent_c = send_ctx([pick(sent, me ^ r) for r in range(nc)])
    sent_z = gather_z(place(sent_c, me_c))
    mine = tokens.reshape(groups, ctx_rows, width)
    inputs_all = []
    for g in range(groups):
        rows_now = after(mine[g], sent_c) if g == 0 else after(mine[g], inputs_all[g - 1])
        inputs_all.append(exchange_ctx(jnp.broadcast_to(rows_now[None], (nc, ctx_rows, width))))
    inputs_all = [t.reshape(length, width) for t in inputs_all]
    sent = place(sent_z, me_z)
    sent = in_order(sent, core_swap(sent), core, 2)
    sent = jnp.moveaxis(sent, 0, 1)
    w_qkv = sent[:, :, :, :rows_w].reshape(width, 3 * cols)
    packed = sent[:, :, :, rows_w:].reshape(nc * nf, 8 * 3 * cols)
    full = [packed[:, j * rows_w : (j + 1) * rows_w].reshape(width) for j in range(8)]
    query_bias, value_bias, out_bias, gain_one, bias_one, down_bias, gain_two, bias_two = full
    up_bias = packed[:, 8 * rows_w : 8 * rows_w + ff_w].reshape(nc * nz, 2, ff_w)
    up_bias = lax.dynamic_index_in_dim(up_bias, core, 1, False).reshape(half)

    split = w_up.reshape(rows_w, half // ff_w, 2, ff_w)
    keep = lax.dynamic_index_in_dim(split, core, 2, False).reshape(rows_w, half)
    give = lax.dynamic_index_in_dim(split, 1 - core, 2, False).reshape(rows_w, half)
    up_mine = in_order(keep, core_swap(give), core, 0).reshape(2 * rows_w, half)
    parts = half // width
    own = jnp.concatenate([up_mine[:, j * width : (j + 1) * width] for j in range(parts)] + [w_down])
    own = lax.all_gather(own, BOTH, axis=0, axis_index_groups=core_groups())

    key_pos = jnp.arange(length, dtype=jnp.int32)
    lengths = doc_lengths.reshape(groups, -1)
    zero_bias = jnp.zeros((cols,), BF)
    qkv_bias = jnp.concatenate(
        [
            lax.dynamic_slice_in_dim(query_bias, me * cols, cols),
            zero_bias,
            lax.dynamic_slice_in_dim(value_bias, me * cols, cols),
        ]
    ).astype(F32)[:, None]
    segs, qkvs, lses = [], [], []
    outs = []
    for g in range(groups):
        segs.append(segment_ids(lengths[g], key_pos))
        rows_now = inputs_all[g] if g == 0 else after(inputs_all[g], outs[0])
        qkvs.append((dot(w_qkv, rows_now, 0, 1) + qkv_bias).astype(BF))
        o, lse = attend(qkvs[g], segs[g], ctx_rows)
        outs.append(o)
        lses.append(lse)
    out_c = send_ctx([place(gather_z(after(w_out, outs[0])), me_z)] * nc)
    out_mat = place(after(out_c, outs[-1]), me_c)
    out_mat = in_order(out_mat, core_swap(out_mat), core, 2).reshape(width, width)
    mixed = exchange_ctx(jnp.concatenate(outs, axis=2))
    own = after(own, mixed)
    mixed = mixed.reshape(width, flat_rows)
    n_up = 2 * rows_w * parts
    up_mat = jnp.concatenate(
        [own[:, j * 2 * rows_w : (j + 1) * 2 * rows_w].reshape(width, width) for j in range(parts)], axis=1
    )
    down_mat = own[:, n_up : n_up + ff_w].reshape(half, width)
    inputs = mine.reshape(flat_rows, width).astype(F32)
    attended = dot(mixed, out_mat, 0, 0) + out_bias
    first, normed_one, inverse_one = norm_forward(inputs + attended, gain_one, bias_one)
    first_low = first.astype(BF)
    both_first = jnp.concatenate([first_low, core_swap(first_low)])
    hidden = dot(both_first, up_mat, 1, 0) + up_bias
    cdf = 0.5 * (1.0 + lax.erf(hidden * 0.7071067811865476))
    slope = (cdf + hidden * jnp.exp(-0.5 * hidden * hidden) * 0.3989422804014327).astype(BF)
    activated = (hidden * cdf).astype(BF)
    away = core_swap(dot(activated[flat_rows:], down_mat, 1, 0).astype(BF))
    branch = dot(activated[:flat_rows], down_mat, 1, 0) + away.astype(F32) + down_bias
    result, normed_two, inverse_two = norm_forward(first + branch, gain_two, bias_two)
    output = result.astype(BF).reshape(micro, per_device, ctx_rows, width)

    upstream = cotangent.reshape(flat_rows, width).astype(F32)
    grad_h2, grad_gain_two, grad_bias_two = norm_backward(upstream, normed_two, inverse_two, gain_two)
    grad_branch = grad_h2.astype(BF)
    grad_down_bias = jnp.sum(grad_branch.astype(F32), axis=0)
    other_branch = core_swap(grad_branch)
    hidden_own = (dot(grad_branch, down_mat, 1, 1) * slope[:flat_rows].astype(F32)).astype(BF)
    grad_down = dot(activated, jnp.concatenate([grad_branch, other_branch]), 0, 0).astype(BF)
    other_branch = lax.optimization_barrier((other_branch, grad_down))[0]
    grad_down = lax.psum_scatter(grad_down, "ctx", scatter_dimension=0, tiled=True)
    hidden_other = (dot(other_branch, down_mat, 1, 1) * slope[flat_rows:].astype(F32)).astype(BF)
    grad_hidden = jnp.concatenate([hidden_own, hidden_other])
    grad_up_bias = dot(jnp.ones((8, grad_hidden.shape[0]), BF), grad_hidden, 1, 0)[0]
    away = core_swap(dot(hidden_other, up_mat, 1, 1).astype(BF))
    grad_first = dot(hidden_own, up_mat, 1, 1) + away.astype(F32) + grad_h2
    grad_h1, grad_gain_one, grad_bias_one = norm_backward(grad_first, normed_one, inverse_one, gain_one)
    grad_attended = grad_h1.astype(BF)
    grad_out_bias = jnp.sum(grad_attended.astype(F32), axis=0)
    do_all = exchange_ctx(dot(out_mat, grad_attended, 1, 1).astype(BF).reshape(nc, cols, flat_rows))
    later = after((both_first, grad_hidden, mixed, grad_attended), do_all)
    grad_out = dot(mixed, grad_attended, 1, 0).astype(BF).reshape(nc, nz, 2, rows_w, width)
    grad_ups = [
        dot(later[0], later[1][:, j * width : (j + 1) * width], 0, 0).astype(BF) for j in range(parts)
    ]
    grad_out_got = core_swap(lax.dynamic_index_in_dim(grad_out, 1 - core, 2, False))
    grad_out = lax.dynamic_index_in_dim(grad_out, core, 2, False).astype(F32) + grad_out_got.astype(F32)
    mats = [t.reshape(nc, nz, 2 * rows_w, width) for t in grad_ups] + [grad_out.astype(BF)]
    grad_up = jnp.concatenate(mats, axis=2).reshape(nc, nz * (n_up + rows_w), width)
    grad_up = lax.psum_scatter(grad_up, "ctx", scatter_dimension=0).reshape(nz, n_up + rows_w, width)

    backs = []
    grad_qkv = None
    grad_bias_parts = []
    for g in range(groups):
        dqkv = attend_back(qkvs[g], do_all, g, lses[g], segs[g], ctx_rows)
        if g == 1:
            dqkv, backs[0], down_got = lax.optimization_barrier((dqkv, backs[0], down_got))
        grad_bias_parts.append(jnp.sum(dqkv.astype(F32), axis=1))
        back = dot(dqkv, w_qkv, 0, 1).astype(BF).reshape(nc, ctx_rows, width)
        if g + 1 < groups:
            grad_down = after(grad_down, dqkv).reshape(nz, ff_w, width)
            down_got = z_send(grad_down)
            qkvs[g + 1] = after(qkvs[g + 1], back)
        if g + 1 < groups:
            backs.append(exchange_ctx(back))
        else:
            backs.append(send_ctx([pick(back, me ^ r) for r in range(nc)]))
        now = dot(inputs_all[g], dqkv, 0, 1)
        grad_qkv = now if grad_qkv is None else grad_qkv + now
    grad_bias = sum(grad_bias_parts).reshape(3, cols)
    spread = lambda v: lax.dynamic_update_slice_in_dim(jnp.zeros((width,), F32), v, me * cols, 0)
    small = [
        spread(grad_bias[0]),
        spread(grad_bias[2]),
        grad_out_bias,
        grad_gain_one,
        grad_bias_one,
        grad_down_bias,
        grad_gain_two,
        grad_bias_two,
    ]
    small = [t.reshape(nc * nf, rows_w) for t in small]
    grad_up_bias = grad_up_bias.reshape(nc * nz, ff_w)
    pair = [jnp.where(core == j, grad_up_bias, 0.0) for j in range(2)]
    small.append(jnp.stack(pair, axis=1).reshape(nc * nf, ff_w))
    small = jnp.concatenate(small, axis=1)
    small = jnp.pad(small, ((0, 0), (0, 8 * 3 * cols - small.shape[1]))).astype(BF)
    small = small.reshape(nc, nz, 2, 8, 3 * cols)
    grad_qkv = grad_qkv.astype(BF).reshape(nc, nz, 2, rows_w, 3 * cols)
    grad_qkv = jnp.concatenate([grad_qkv, small], axis=3)
    grad_qkv_got = core_swap(lax.dynamic_index_in_dim(grad_qkv, 1 - core, 2, False))
    grad_qkv = lax.dynamic_index_in_dim(grad_qkv, core, 2, False).astype(F32) + grad_qkv_got.astype(F32)
    grad_qkv = jnp.moveaxis(grad_qkv.astype(BF), 1, 0)
    grad_qkv = z_sum(grad_qkv, z_send(grad_qkv)).astype(BF)
    backs[-1] = after(backs[-1], grad_qkv)
    got = send_ctx([pick(grad_qkv, me ^ r) for r in range(nc)])
    small = total_of([t[rows_w:] for t in got]).reshape(8 * 3 * cols)
    grad_qkv = place([t[:rows_w] for t in got], me_c).reshape(nc, rows_w, 3, cols)
    grad_qkv = jnp.moveaxis(grad_qkv, 0, 2).reshape(rows_w, 3, width).astype(F32)
    grad_up = lax.psum_scatter(grad_up, "fsdp", scatter_dimension=0, axis_index_groups=z_groups())
    input_grads = [total_of([t[r] for r in range(nc)]) for t in backs]
    grad_down = z_sum(grad_down, down_got)
    grad_out = grad_up[n_up:].astype(F32)
    grad_up = [grad_up[j * 2 * rows_w : (j + 1) * 2 * rows_w] for j in range(parts)]
    grad_up = jnp.concatenate(grad_up, axis=1).reshape(2, rows_w, half)
    grad_up_got = core_swap(lax.dynamic_index_in_dim(grad_up, 1 - core, 0, False))
    pair = [
        t.reshape(rows_w, half // ff_w, ff_w)
        for t in (lax.dynamic_index_in_dim(grad_up, core, 0, False), grad_up_got)
    ]
    grad_up = in_order(pair[0], pair[1], core, 2).reshape(rows_w, ff).astype(F32)
    grad_tokens = grad_h1.reshape(groups, ctx_rows, width) + jnp.stack(input_grads)
    grad_tokens = grad_tokens.reshape(micro, per_device, ctx_rows, width)

    small_out = [small[j * rows_w : (j + 1) * rows_w] for j in range(8)]
    g_bq, g_bv, g_bo, g_g1, g_b1, g_bd, g_g2, g_b2 = small_out
    g_bu = small[8 * rows_w : 8 * rows_w + ff_w]

    return (
        output,
        grad_tokens,
        grad_qkv[:, 0],
        g_bq,
        grad_qkv[:, 1],
        grad_qkv[:, 2],
        g_bv,
        grad_out,
        g_bo,
        g_g1,
        g_b1,
        grad_up,
        g_bu,
        grad_down,
        g_bd,
        g_g2,
        g_b2,
    )


def solution(mesh):
    stream = P(None, "fsdp", "ctx", None)
    mat = P(BOTH, None)
    vec = P(BOTH)
    return jax.shard_map(
        body,
        mesh=mesh,
        in_specs=(
            stream,
            P(None, "fsdp", None),
            mat,
            vec,
            mat,
            mat,
            vec,
            mat,
            vec,
            vec,
            vec,
            mat,
            vec,
            mat,
            vec,
            vec,
            vec,
            stream,
        ),
        out_specs=(
            stream,
            stream,
            mat,
            vec,
            mat,
            mat,
            vec,
            mat,
            vec,
            vec,
            vec,
            mat,
            vec,
            mat,
            vec,
            vec,
            vec,
        ),
        check_vma=False,
    )
```
